128 devices in a mesh: plane: 4 (over x_hi, core), ray: 32 (over z, y, x_lo).
Axes of the slice: x: 4 (x_hi: 2, x_lo: 2; x = x_hi * 2 + x_lo), y: 4, z: 4, core: 2. Of those that a mesh axis runs over, the one named last changes fastest.
Arguments:
- coarse_potential: float32 [2048, 512], P(('plane', 'ray')), may hold values from -72 to 72
- fine_tiles: bfloat16 [4, 32768, 256], P('plane', 'ray'), may hold values from -0.59765625 to 0.59765625
- tile_requests: int32 [128, 4, 32, 16], P(('plane', 'ray')), may hold values from 0 to 1023, as said below
- ray_slot: int32 [4, 131072], P(None, ('plane', 'ray')), may hold values from 0 to 511, as said below
- fine_cell: int32 [4, 131072], P(None, ('plane', 'ray')), may hold values from 17 to 221, as said below
- coarse_cell: int32 [4, 131072], P(None, ('plane', 'ray')), may hold values from 0 to 262143
- tile_root: int32 [4, 131072], P(None, ('plane', 'ray')), may hold values from 0 to 3
- ray_offset: float32 [2, 131072], P(None, ('plane', 'ray')), may hold values from 0 to 1
Outputs:
- displacement: float32 [2, 131072], P(None, ('plane', 'ray'))
- distortion: float32 [4, 131072], P(None, ('plane', 'ray'))
The draws below stay inside these ranges and needn't reach their ends.
Inputs may be any that keep to these rules, and one draw needn't show every extreme that they name: `tile_requests`: entries are tile indices within one owner's tiles of the plane. `ray_slot`: A ray's slot r * 16 + s names a tile requested by its own bundle from owner r at that plane. `fine_cell`: both coordinates of a ray's fine cell lie in 1 to 13.
All inputs are finite; a program needn't handle non-finite values.
Results may differ from the reference program's by a relative error of at most 0.0026.
Values may be sent and summed in bfloat16 or wider, within the bound.
No kernel may reach another device: no remote copies, remote signals or barrier semaphores. Data moves between devices by JAX's collectives and lax.ppermute only.
A program may use at most 128 MiB of HBM per device.

```python
import jax
import jax.numpy as jnp
from jax import lax

TP = 16
CG = 512
RATIO = 32
FIRST = 31
SLOT = 16
RAYS_DEV = 1024
TILES_DEV = 1024
PLANES = 4
OWNERS = 32
BUNDLES = 128
TILES = 32768
RAYS = 131072


def slot_counts(key):
    base_key = jax.random.fold_in(key, 97)
    first_key, second_key = jax.random.split(base_key)
    shifts = jax.random.randint(first_key, (BUNDLES, PLANES, OWNERS), 0, 4).astype(jnp.int32)
    filled = jnp.full((BUNDLES, PLANES, OWNERS), SLOT, jnp.int32)
    counts = jnp.maximum(jnp.right_shift(filled, shifts), 1)
    fullest = jax.random.randint(second_key, (BUNDLES, PLANES, 1), 0, OWNERS).astype(jnp.int32)
    owner_ids = jnp.arange(OWNERS, dtype=jnp.int32)[None, None, :]
    return jnp.where(owner_ids == fullest, SLOT, counts).astype(jnp.int32)


def draw_tile_requests(key, part):
    base_key = jax.random.fold_in(key, 11)
    first_key, second_key = jax.random.split(base_key)
    raw_ids = jax.random.randint(first_key, (BUNDLES, PLANES, OWNERS, SLOT), 0, TILES_DEV).astype(jnp.int32)
    shifts = jax.random.randint(second_key, (BUNDLES, PLANES, OWNERS, SLOT), 0, 6).astype(jnp.int32)
    return jnp.right_shift(raw_ids, shifts)


def draw_ray_slot(key, part):
    counts = slot_counts(key)
    base_key = jax.random.fold_in(key, 211)
    owner_key, within_key = jax.random.split(base_key)
    owner = jax.random.randint(owner_key, (PLANES, RAYS), 0, OWNERS).astype(jnp.int32)
    bundle = jnp.arange(RAYS, dtype=jnp.int32) // RAYS_DEV
    plane_ids = jnp.arange(PLANES, dtype=jnp.int32)[:, None]
    live = counts[bundle[None, :], plane_ids, owner]
    within = jax.random.randint(within_key, (PLANES, RAYS), 0, live).astype(jnp.int32)
    return owner * SLOT + within


def draw_fine_cell(key, part):
    base_key = jax.random.fold_in(key, 331)
    first_key, second_key = jax.random.split(base_key)
    cell_x = jax.random.randint(first_key, (PLANES, RAYS), 1, TP - 2).astype(jnp.int32)
    cell_y = jax.random.randint(second_key, (PLANES, RAYS), 1, TP - 2).astype(jnp.int32)
    return cell_y * TP + cell_x


def plant(result, rng, least, largest):
    longest = result.shape.index(max(result.shape))
    spots = []
    for shift in (0, 1):
        where = [jax.random.randint(jax.random.fold_in(rng, axis), (), 0, length) for axis, length in enumerate(result.shape)]
        where[longest] = (where[longest] + shift) % result.shape[longest]
        spots.append(tuple(where))
    return result.at[spots[0]].set(least).at[spots[1]].set(largest)


def shard_levels(own_key, extent, cuts, low, largest):
    def one(dim, shards_of):
        heights = jax.random.uniform(jax.random.fold_in(jax.random.fold_in(own_key, 6), dim), (shards_of,), jnp.float32, low / len(cuts), largest / len(cuts))
        return jnp.repeat(jnp.exp(heights), extent[dim] // shards_of).reshape((-1,) + (1,) * (len(extent) - dim - 1))

    factor_of = one(*cuts[0])
    for cut in cuts[1:]:
        factor_of = factor_of * one(*cut)
    return factor_of


def gaussian(rng, dims, scale, most, shards=(), kind=jnp.bfloat16):
    values = scale * jax.random.normal(rng, dims, jnp.float32)
    if shards:
        values = values * shard_levels(rng, dims, shards, -0.22, 0.18)
    return jnp.clip(values, -most, most).astype(kind)


def setup_inputs(seed: int = 0) -> dict:
    key_of = jax.random.split(jax.random.key(seed), 9)
    return {
        "coarse_potential": gaussian(key_of[0], (PLANES * CG, CG), 12.0, 72.0, ((0, 128),), jnp.float32),
        "fine_tiles": gaussian(key_of[1], (PLANES, TILES, TP * TP), 0.1, 0.59765625, ((0, 4), (1, 32))),
        "tile_requests": draw_tile_requests(jax.random.fold_in(key_of[8], 71), 0),
        "ray_slot": draw_ray_slot(jax.random.fold_in(key_of[8], 71), 0),
        "fine_cell": draw_fine_cell(jax.random.fold_in(key_of[8], 71), 0),
        "coarse_cell": plant(jax.random.randint(key_of[5], (PLANES, RAYS), 0, CG * CG), jax.random.fold_in(key_of[5], 1), 0, (CG * CG) - 1).astype(jnp.int32),
        "tile_root": plant(jax.random.randint(key_of[6], (PLANES, RAYS), 0, 4), jax.random.fold_in(key_of[6], 1), 0, 3).astype(jnp.int32),
        "ray_offset": jnp.clip(1.0 * jax.random.uniform(key_of[7], (2, RAYS), jnp.float32) ** shard_levels(key_of[7], (2, RAYS), ((1, 128),), -0.2, 0.2), 0.0, 1.0),
    }


def tile_fields(tiles):
    padded = jnp.pad(tiles, ((0, 0), (1, 1), (1, 1)))
    middle = tiles
    right_val = padded[:, 1:-1, 2:]
    left_val = padded[:, 1:-1, :-2]
    upper_val = padded[:, 2:, 1:-1]
    lower_val = padded[:, :-2, 1:-1]
    grad_x = (right_val - left_val) * 0.5
    grad_y = (upper_val - lower_val) * 0.5
    hess_xx = right_val - 2.0 * middle + left_val
    hess_yy = upper_val - 2.0 * middle + lower_val
    hess_xy = (padded[:, 2:, 2:] - padded[:, :-2, 2:] - padded[:, 2:, :-2] + padded[:, :-2, :-2]) * 0.25
    return jnp.stack([grad_x, grad_y, hess_xx, hess_yy, hess_xy], axis=1)


def coarse_terms(plane_flat, coarse_row, fine_row, root_row, position, coarse_side):
    cell_x = coarse_row % coarse_side
    cell_y = coarse_row // coarse_side
    root_x = ((root_row % 2) * (RATIO // 2)).astype(jnp.float32)
    root_y = ((root_row // 2) * (RATIO // 2)).astype(jnp.float32)
    frac_x = (root_x + (fine_row % TP).astype(jnp.float32) + position[0]) / RATIO
    frac_y = (root_y + (fine_row // TP).astype(jnp.float32) + position[1]) / RATIO
    grid_rows = []
    for shift_y in range(-1, 3):
        row_base = ((cell_y + shift_y) % coarse_side) * coarse_side
        grid_rows.append([jnp.take(plane_flat, row_base + (cell_x + shift_x) % coarse_side) for shift_x in range(-1, 3)])
    weights = [(1.0 - frac_x) * (1.0 - frac_y), frac_x * (1.0 - frac_y), (1.0 - frac_x) * frac_y, frac_x * frac_y]
    total = jnp.zeros((5, coarse_row.shape[0]), jnp.float32)
    corner_list = ((0, 0), (0, 1), (1, 0), (1, 1))
    for corner_index in range(4):
        step_y = corner_list[corner_index][0] + 1
        step_x = corner_list[corner_index][1] + 1
        middle = grid_rows[step_y][step_x]
        right_val = grid_rows[step_y][step_x + 1]
        left_val = grid_rows[step_y][step_x - 1]
        upper_val = grid_rows[step_y + 1][step_x]
        lower_val = grid_rows[step_y - 1][step_x]
        cross = (grid_rows[step_y + 1][step_x + 1] - grid_rows[step_y - 1][step_x + 1] - grid_rows[step_y + 1][step_x - 1] + grid_rows[step_y - 1][step_x - 1]) * 0.25
        stacked = jnp.stack([(right_val - left_val) * 0.5, (upper_val - lower_val) * 0.5, right_val - 2.0 * middle + left_val, upper_val - 2.0 * middle + lower_val, cross])
        total = total + weights[corner_index] * stacked
    scales = jnp.array([1.0 / RATIO, 1.0 / RATIO, 1.0 / (RATIO * RATIO), 1.0 / (RATIO * RATIO), 1.0 / (RATIO * RATIO)], jnp.float32)
    return total * scales[:, None]


def advance(displacement, previous, distortion, before, deriv, plane_index):
    chi_now = float(FIRST + plane_index)
    ahead = 2.0 * chi_now / (chi_now + 1.0)
    behind = (chi_now - 1.0) / (chi_now + 1.0)
    strength = chi_now / (chi_now + 1.0)
    grad_x, grad_y, hess_xx, hess_yy, hess_xy = deriv[0], deriv[1], deriv[2], deriv[3], deriv[4]
    new_disp = ahead * displacement - behind * previous - strength * jnp.stack([grad_x, grad_y])
    product = jnp.stack([hess_xx * distortion[0] + hess_xy * distortion[2], hess_xx * distortion[1] + hess_xy * distortion[3], hess_xy * distortion[0] + hess_yy * distortion[2], hess_xy * distortion[1] + hess_yy * distortion[3]])
    new_dist = ahead * distortion - behind * before - strength * product
    return new_disp, displacement, new_dist, distortion


def reference(coarse_potential, fine_tiles, tile_requests, ray_slot, fine_cell, coarse_cell, tile_root, ray_offset):
    planes = fine_tiles.shape[0]
    owners = tile_requests.shape[2]
    bundles = tile_requests.shape[0]
    coarse_side = coarse_potential.shape[1]
    count_rays = ray_offset.shape[1]
    per_bundle = count_rays // bundles
    tiles_per = fine_tiles.shape[1] // owners
    tile_cells = TP * TP
    displacement = jnp.zeros((2, count_rays), jnp.float32)
    previous = displacement
    ones_row = jnp.ones((count_rays,), jnp.float32)
    zero_row = jnp.zeros((count_rays,), jnp.float32)
    distortion = jnp.stack([ones_row, zero_row, zero_row, ones_row])
    before = distortion
    for plane_index in range(planes):
        position = ray_offset + displacement
        plane_flat = coarse_potential[plane_index * coarse_side:(plane_index + 1) * coarse_side].reshape(-1)
        coarse_part = coarse_terms(plane_flat, coarse_cell[plane_index], fine_cell[plane_index], tile_root[plane_index], position, coarse_side)
        plane_tiles = fine_tiles[plane_index]

        def per_bundle_fn(pieces):
            requests, slot_row, cell_row, pos_rows = pieces
            tile_ids = (jnp.arange(owners, dtype=jnp.int32)[:, None] * tiles_per + requests).reshape(-1)
            tiles = plane_tiles[tile_ids].reshape(-1, TP, TP).astype(jnp.float32)
            rounded = lax.optimization_barrier(tile_fields(tiles).astype(jnp.bfloat16))
            fields = rounded.astype(jnp.float32).reshape(-1, 5, tile_cells)
            chosen = fields[slot_row]
            along_x = pos_rows[0]
            along_y = pos_rows[1]

            def corner(offset):
                return jnp.take_along_axis(chosen, (cell_row + offset)[:, None, None], axis=2)[:, :, 0].T

            return ((1.0 - along_x) * (1.0 - along_y) * corner(0) + along_x * (1.0 - along_y) * corner(1)
                    + (1.0 - along_x) * along_y * corner(TP) + along_x * along_y * corner(TP + 1))

        fine_blocks = lax.map(per_bundle_fn, (tile_requests[:, plane_index], ray_slot[plane_index].reshape(bundles, per_bundle), fine_cell[plane_index].reshape(bundles, per_bundle), position.reshape(2, bundles, per_bundle).transpose(1, 0, 2)))
        fine_part = fine_blocks.transpose(1, 0, 2).reshape(5, count_rays)
        displacement, previous, distortion, before = advance(displacement, previous, distortion, before, fine_part + coarse_part, plane_index)
    return displacement, distortion
```

```python
import jax
import jax.numpy as jnp
from jax import lax
from jax.experimental import pallas as pl
from jax.experimental.pallas import tpu as pltpu
from jax.sharding import PartitionSpec as P

TP = 16
RATIO = 32
FIRST = 31
LANES = 128
HALO = 8
WIN = 8
TALL = WIN + 3


def shift_rows(rows, amount, bits, keep):
    left = sum(bits)
    for bit in bits:
        left -= bit
        taken = (amount & bit) != 0
        need = keep + left
        rows = [
            jnp.where(taken, rows[j + bit], rows[j]) if j + bit < len(rows) else rows[j]
            for j in range(min(need, len(rows)))
        ]
    return rows


def shift_within(low, high, amount):
    index = lax.broadcasted_iota(jnp.int32, low.shape, 0)
    far = jnp.where(index < 4, pltpu.roll(low, 4, 0), pltpu.roll(high, 4, 0))
    here = jnp.where((amount & 4) != 0, far, low)
    here = jnp.where((amount & 2) != 0, pltpu.roll(here, 6, 0), here)
    return jnp.where((amount & 1) != 0, pltpu.roll(here, 7, 0), here)


def out_side(rows):
    side = 1
    while side * side < rows * LANES:
        side *= 2
    return side


def coarse_kernel(plane_ref, cell_ref, out_ref, table_ref):
    side = out_side(plane_ref.shape[0])
    windows = side // WIN
    chunks = side // LANES
    stride = chunks * WIN
    width = TALL * LANES
    step = 256
    count = windows * chunks
    for chunk in range(chunks):
        base = chunk * windows
        after = (chunk + 1) % chunks
        halo = jnp.zeros((windows, LANES), jnp.float32)
        lane = lax.broadcasted_iota(jnp.int32, (windows, LANES), 1)
        for dy in range(TALL):
            row = dy % WIN
            main = plane_ref[pl.ds(chunk * WIN + row, windows, stride=stride), :]
            near = plane_ref[pl.ds(after * WIN + row, windows, stride=stride), :]
            if dy >= WIN:
                main = pltpu.roll(main, windows - 1, 0)
                near = pltpu.roll(near, windows - 1, 0)
            near = pltpu.roll(near, dy * HALO, 1) if dy else near
            halo = jnp.where((lane >= dy * HALO) & (lane < (dy + 1) * HALO), near, halo)
            high = main.astype(jnp.bfloat16)
            low = (main - high.astype(jnp.float32)).astype(jnp.bfloat16)
            table_ref[pl.ds(base, windows), pl.ds(dy * LANES, LANES)] = high
            table_ref[pl.ds(count + base, windows), pl.ds(dy * LANES, LANES)] = low
        high = halo.astype(jnp.bfloat16)
        low = (halo - high.astype(jnp.float32)).astype(jnp.bfloat16)
        table_ref[pl.ds(base, windows), pl.ds(width, LANES)] = high
        table_ref[pl.ds(count + base, windows), pl.ds(width, LANES)] = low

    bundles = cell_ref.shape[0]
    per = cell_ref.shape[1] // step

    def one(index, carry):
        bundle = index // per
        start = pl.multiple_of((index % per) * step, step)
        cell = cell_ref[pl.ds(bundle, 1), pl.ds(start, step)]
        first_x = (cell - 1) & (side - 1)
        first_y = (cell // side - 1) & (side - 1)
        window = (first_x // LANES) * windows + first_y // WIN
        ids = lax.broadcasted_iota(jnp.int32, (count, step), 0)
        onehot = (ids == window).astype(jnp.float32).astype(jnp.bfloat16)
        onehot = jnp.concatenate([onehot, onehot], axis=0)
        picked = lax.dot_general(
            table_ref[...], onehot, (((0,), (0,)), ((), ())), preferred_element_type=jnp.float32
        )
        off_y = first_y & (WIN - 1)
        off_x = first_x & (LANES - 1)
        lines = []
        for dy in range(TALL):
            parts = [picked[dy * LANES + 8 * k : dy * LANES + 8 * k + 8] for k in range(LANES // 8)]
            parts.append(picked[width + dy * HALO : width + (dy + 1) * HALO])
            lines.append(shift_rows(parts, off_x // 8, (8, 4, 2, 1), 2))
        low = shift_rows([line[0] for line in lines], off_y, (4, 2, 1), 4)
        high = shift_rows([line[1] for line in lines], off_y, (4, 2, 1), 4)
        patch = [shift_within(low[i], high[i], off_x)[:4] for i in range(4)]
        out_ref[bundle, :, pl.ds(start, step)] = jnp.concatenate(patch, axis=0)
        return carry

    lax.fori_loop(0, bundles * per, one, 0)


def stencil_terms(patch, frac_x, frac_y):
    keep_y = 1.0 - frac_y
    level = keep_y * patch[1] + frac_y * patch[2]
    slope = (keep_y * (patch[2] - patch[0]) + frac_y * (patch[3] - patch[1])) * 0.5
    bend = keep_y * (patch[2] - 2.0 * patch[1] + patch[0]) + frac_y * (patch[3] - 2.0 * patch[2] + patch[1])
    keep_x = 1.0 - frac_x

    def across(rows):
        return [rows[k : k + 1] for k in range(4)]

    def flat(rows):
        return keep_x * rows[1] + frac_x * rows[2]

    def tilt(rows):
        return (keep_x * (rows[2] - rows[0]) + frac_x * (rows[3] - rows[1])) * 0.5

    def curve(rows):
        return keep_x * (rows[2] - 2.0 * rows[1] + rows[0]) + frac_x * (rows[3] - 2.0 * rows[2] + rows[1])

    level, slope, bend = across(level), across(slope), across(bend)
    return tilt(level), flat(slope), curve(level), flat(bend), tilt(slope)


def trace_kernel(tile_ref, slot_ref, fine_ref, root_ref, coarse_ref, offset_ref, disp_ref, dist_ref, patch_ref):
    planes = tile_ref.shape[0]
    slots = tile_ref.shape[1]
    rays = slot_ref.shape[1]
    step = 256

    def one(index, carry):
        plane = index // (rays // step)
        start = pl.multiple_of((index % (rays // step)) * step, step)
        slot = slot_ref[pl.ds(plane, 1), pl.ds(start, step)]
        cell = fine_ref[pl.ds(plane, 1), pl.ds(start, step)]
        ids = lax.broadcasted_iota(jnp.int32, (slots, step), 0)
        onehot = (ids == slot).astype(jnp.float32).astype(jnp.bfloat16)
        picked = lax.dot_general(
            tile_ref[plane], onehot, (((0,), (0,)), ((), ())), preferred_element_type=jnp.float32
        )
        off_x = cell % TP - 1
        off_y = cell // TP - 1
        low = shift_rows([picked[TP * y : TP * y + 8] for y in range(TP)], off_y, (8, 4, 2, 1), 4)
        high = shift_rows([picked[TP * y + 8 : TP * y + 16] for y in range(TP)], off_y, (8, 4, 2, 1), 4)
        for i in range(4):
            first = jnp.where(off_x >= 8, high[i], low[i])
            patch_ref[plane, i, :, pl.ds(start, step)] = shift_within(first, high[i], off_x)
        return carry

    lax.fori_loop(0, planes * (rays // step), one, 0)

    offset = [offset_ref[0:1], offset_ref[1:2]]
    disp = [jnp.zeros((1, rays), jnp.float32)] * 2
    last = disp
    zero = jnp.zeros((1, rays), jnp.float32)
    unit = jnp.ones((1, rays), jnp.float32)
    dist = [unit, zero, zero, unit]
    before = dist
    for plane in range(planes):
        chi = float(FIRST + plane)
        ahead = 2.0 * chi / (chi + 1.0)
        behind = (chi - 1.0) / (chi + 1.0)
        strength = chi / (chi + 1.0)
        position = [offset[0] + disp[0], offset[1] + disp[1]]
        fine = stencil_terms([patch_ref[plane, i] for i in range(4)], position[0], position[1])
        cell = fine_ref[plane : plane + 1]
        root = root_ref[plane : plane + 1]
        base_x = ((root % 2) * (RATIO // 2) + cell % TP).astype(jnp.float32)
        base_y = ((root // 2) * (RATIO // 2) + cell // TP).astype(jnp.float32)
        coarse = stencil_terms(
            [coarse_ref[plane, 4 * i : 4 * i + 4] for i in range(4)],
            (base_x + position[0]) * (1.0 / RATIO),
            (base_y + position[1]) * (1.0 / RATIO),
        )
        once = 1.0 / RATIO
        twice = once * once
        grad_x = fine[0] + coarse[0] * once
        grad_y = fine[1] + coarse[1] * once
        xx = fine[2] + coarse[2] * twice
        yy = fine[3] + coarse[3] * twice
        xy = fine[4] + coarse[4] * twice
        new_disp = [
            ahead * disp[0] - behind * last[0] - strength * grad_x,
            ahead * disp[1] - behind * last[1] - strength * grad_y,
        ]
        product = [
            xx * dist[0] + xy * dist[2],
            xx * dist[1] + xy * dist[3],
            xy * dist[0] + yy * dist[2],
            xy * dist[1] + yy * dist[3],
        ]
        new_dist = [ahead * dist[k] - behind * before[k] - strength * product[k] for k in range(4)]
        disp, last, dist, before = new_disp, disp, new_dist, dist
    for k in range(2):
        disp_ref[k : k + 1] = disp[k]
    for k in range(4):
        dist_ref[k : k + 1] = dist[k]


def swap(array, axes):
    return lax.all_to_all(array, axes, split_axis=0, concat_axis=0, tiled=True)


def body(
    coarse_potential,
    fine_tiles,
    tile_requests,
    ray_slot,
    fine_cell,
    coarse_cell,
    tile_root,
    ray_offset,
):
    planes = lax.axis_size("plane")
    owners = lax.axis_size("ray")
    slots = tile_requests.shape[3]
    side = coarse_potential.shape[1]
    rays = ray_offset.shape[1]
    cells = TP * TP
    wanted = swap(tile_requests.reshape(planes * owners, slots), ("plane", "ray"))

    chunks = side // LANES
    rows = coarse_potential.reshape(-1, WIN, chunks, LANES).transpose(0, 2, 1, 3).reshape(-1, LANES)
    rows = jnp.broadcast_to(rows[None], (owners,) + rows.shape)
    plane_rows = swap(rows, "ray").reshape(side * chunks, LANES)
    asked = swap(coarse_cell, "plane")
    found = pl.pallas_call(
        coarse_kernel,
        out_shape=jax.ShapeDtypeStruct((planes, 16, rays), jnp.float32),
        in_specs=[pl.BlockSpec(memory_space=pltpu.VMEM)] * 2,
        out_specs=pl.BlockSpec(memory_space=pltpu.VMEM),
        scratch_shapes=[pltpu.VMEM((2 * side // WIN * (side // LANES), (TALL + 1) * LANES), jnp.bfloat16)],
        compiler_params=pltpu.CompilerParams(vmem_limit_bytes=32 << 20),
        cost_estimate=pl.CostEstimate(flops=6_000_000_000, bytes_accessed=1_500_000, transcendentals=0),
        name="coarse",
    )(plane_rows, asked)
    coarse = swap(found, "plane")

    outgoing = fine_tiles[0].at[wanted.reshape(-1)].get(mode="promise_in_bounds")
    arrived = swap(outgoing.reshape(planes * owners, slots, cells), ("plane", "ray"))
    return pl.pallas_call(
        trace_kernel,
        out_shape=(
            jax.ShapeDtypeStruct((2, rays), jnp.float32),
            jax.ShapeDtypeStruct((4, rays), jnp.float32),
        ),
        in_specs=[pl.BlockSpec(memory_space=pltpu.VMEM)] * 6,
        out_specs=(pl.BlockSpec(memory_space=pltpu.VMEM),) * 2,
        scratch_shapes=[pltpu.VMEM((planes, 4, 8, rays), jnp.float32)],
        compiler_params=pltpu.CompilerParams(vmem_limit_bytes=32 << 20),
        cost_estimate=pl.CostEstimate(flops=1_500_000_000, bytes_accessed=1_500_000, transcendentals=0),
        name="trace",
    )(
        arrived.reshape(planes, owners * slots, cells),
        ray_slot,
        fine_cell,
        tile_root,
        coarse,
        ray_offset,
    )


def solution(mesh):
    in_specs = (
        P(("plane", "ray"), None),
        P("plane", "ray", None),
        P(("plane", "ray"), None, None, None),
        P(None, ("plane", "ray")),
        P(None, ("plane", "ray")),
        P(None, ("plane", "ray")),
        P(None, ("plane", "ray")),
        P(None, ("plane", "ray")),
    )
    out_specs = (P(None, ("plane", "ray")), P(None, ("plane", "ray")))
    return jax.shard_map(body, mesh=mesh, in_specs=in_specs, out_specs=out_specs, check_vma=False)
```

```python
import jax
import jax.numpy as jnp
from jax import lax
from jax.experimental import pallas as pl
from jax.experimental.pallas import tpu as pltpu
from jax.sharding import PartitionSpec as P

TP = 16
RATIO = 32
FIRST = 31
LANES = 128
HALO = 8
WIN = 8
TALL = WIN + 3
UNIT = 72.0 / 32767.0


def shift_rows(rows, amount, bits, keep):
    left = sum(bits)
    for bit in bits:
        left -= bit
        taken = (amount & bit) != 0
        need = keep + left
        rows = [
            jnp.where(taken, rows[j + bit], rows[j]) if j + bit < len(rows) else rows[j]
            for j in range(min(need, len(rows)))
        ]
    return rows


def shift_within(low, high, amount):
    index = lax.broadcasted_iota(jnp.int32, low.shape, 0)
    far = jnp.where(index < 4, pltpu.roll(low, 4, 0), pltpu.roll(high, 4, 0))
    here = jnp.where((amount & 4) != 0, far, low)
    here = jnp.where((amount & 2) != 0, pltpu.roll(here, 6, 0), here)
    return jnp.where((amount & 1) != 0, pltpu.roll(here, 7, 0), here)


def pack_kernel(coarse_ref, request_ref, out_ref, row_ref):
    planes, owners, slots = request_ref.shape
    side = coarse_ref.shape[1]
    half = side // 2
    code = jnp.floor(coarse_ref[...] * (1.0 / UNIT) + 0.5).astype(jnp.int32)
    word = (code[:, :half] << 16) | (code[:, half:] & 0xFFFF)
    tiles = []
    for y in range(coarse_ref.shape[0] // WIN):
        for x in range(half // LANES):
            tiles.append(word[y * WIN : (y + 1) * WIN, x * LANES : (x + 1) * LANES])
    block = jnp.concatenate(tiles, axis=0)
    row_ref[...] = jnp.zeros_like(row_ref)
    for plane in range(planes):
        row_ref[:, plane * slots : (plane + 1) * slots] = request_ref[plane]
    size = block.shape[0]
    for owner in range(owners):
        out_ref[owner, 0:size] = block
        out_ref[owner, size : size + 8] = jnp.broadcast_to(row_ref[owner : owner + 1], (8, LANES))


def take_kernel(plane_ref, own_ref, one_ref, two_ref, three_ref, tile_ref, out_ref, turned_ref):
    planes, owners, slots, cells = out_ref.shape
    plane = plane_ref[0]
    count = tile_ref.shape[0]
    group = 16
    ids = lax.broadcasted_iota(jnp.int32, (slots, count), 1)
    for k, ref in enumerate((own_ref, one_ref, two_ref, three_ref)):
        turned_ref[...] = jnp.transpose(ref[...])
        wanted = turned_ref[pl.ds(pl.multiple_of(plane * slots, slots), slots), :]
        source = (plane + planes - k) & (planes - 1)
        for first in range(0, owners, group):
            onehot = jnp.concatenate(
                [(ids == wanted[:, r : r + 1]).astype(jnp.float32).astype(jnp.bfloat16) for r in range(first, first + group)],
                axis=0,
            )
            got = jnp.dot(onehot, tile_ref[...], preferred_element_type=jnp.float32).astype(jnp.bfloat16)
            out_ref[source, pl.ds(first, group)] = got.reshape(group, slots, cells)


def coarse_kernel(plane_ref, grid_ref, own_ref, one_ref, two_ref, three_ref, out_ref, table_ref, cell_ref):
    owners, rows, _ = grid_ref.shape
    plane = plane_ref[0]
    side = owners * 2 * WIN
    windows = side // WIN
    chunks = side // LANES
    halves = chunks // 2
    width = TALL * LANES
    step = 256
    count = windows * chunks
    grid = grid_ref.reshape(owners * rows, LANES)

    def load(chunk, dy):
        parts = []
        for parity in range(2):
            pick = (parity + dy // WIN) % 2
            start = (pick * halves + chunk % halves) * WIN + dy % WIN
            part = grid[pl.ds(start, owners, stride=rows), :]
            if parity + dy // WIN >= 2:
                part = pltpu.roll(part, owners - 1, 0)
            parts.append(part)
        word = jnp.concatenate(parts, axis=0)
        return word >> 16 if chunk < halves else (word << 16) >> 16

    def put(code, start, column):
        high = ((code + 128) >> 8) << 8
        table_ref[pl.ds(start, windows), pl.ds(column, LANES)] = high.astype(jnp.float32).astype(jnp.bfloat16)
        table_ref[pl.ds(count + start, windows), pl.ds(column, LANES)] = (
            (code - high).astype(jnp.float32).astype(jnp.bfloat16)
        )

    lane = lax.broadcasted_iota(jnp.int32, (windows, LANES), 1)
    for chunk in range(chunks):
        base = chunk * windows
        halo = jnp.zeros((windows, LANES), jnp.int32)
        for dy in range(TALL):
            near = load((chunk + 1) % chunks, dy)
            near = pltpu.roll(near, dy * HALO, 1) if dy else near
            halo = jnp.where((lane >= dy * HALO) & (lane < (dy + 1) * HALO), near, halo)
            put(load(chunk, dy), base, dy * LANES)
        put(halo, base, width)

    for k, ref in enumerate((own_ref, one_ref, two_ref, three_ref)):
        cell_ref[k : k + 1] = ref[pl.ds(plane, 1), :]

    bundles = cell_ref.shape[0]
    per = cell_ref.shape[1] // step

    def one(index, carry):
        bundle = index // per
        start = pl.multiple_of((index % per) * step, step)
        cell = cell_ref[pl.ds(bundle, 1), pl.ds(start, step)]
        first_x = (cell - 1) & (side - 1)
        first_y = (cell // side - 1) & (side - 1)
        tall = first_y // WIN
        window = (first_x // LANES) * windows + (tall & 1) * owners + tall // 2
        ids = lax.broadcasted_iota(jnp.int32, (count, step), 0)
        onehot = (ids == window).astype(jnp.float32).astype(jnp.bfloat16)
        onehot = jnp.concatenate([onehot, onehot], axis=0)
        picked = lax.dot_general(
            table_ref[...], onehot, (((0,), (0,)), ((), ())), preferred_element_type=jnp.float32
        )
        off_y = first_y & (WIN - 1)
        off_x = first_x & (LANES - 1)
        lines = []
        for dy in range(TALL):
            parts = [picked[dy * LANES + 8 * k : dy * LANES + 8 * k + 8] for k in range(LANES // 8)]
            parts.append(picked[width + dy * HALO : width + (dy + 1) * HALO])
            lines.append(shift_rows(parts, off_x // 8, (8, 4, 2, 1), 2))
        low = shift_rows([line[0] for line in lines], off_y, (4, 2, 1), 4)
        high = shift_rows([line[1] for line in lines], off_y, (4, 2, 1), 4)
        patch = [shift_within(low[i], high[i], off_x)[:4] for i in range(4)]
        out_ref[bundle, :, pl.ds(start, step)] = jnp.concatenate(patch, axis=0)
        return carry

    lax.fori_loop(0, bundles * per, one, 0)


def stencil_terms(patch, frac_x, frac_y):
    keep_y = 1.0 - frac_y
    level = keep_y * patch[1] + frac_y * patch[2]
    slope = (keep_y * (patch[2] - patch[0]) + frac_y * (patch[3] - patch[1])) * 0.5
    bend = keep_y * (patch[2] - 2.0 * patch[1] + patch[0]) + frac_y * (patch[3] - 2.0 * patch[2] + patch[1])
    keep_x = 1.0 - frac_x

    def across(rows):
        return [rows[k : k + 1] for k in range(4)]

    def flat(rows):
        return keep_x * rows[1] + frac_x * rows[2]

    def tilt(rows):
        return (keep_x * (rows[2] - rows[0]) + frac_x * (rows[3] - rows[1])) * 0.5

    def curve(rows):
        return keep_x * (rows[2] - 2.0 * rows[1] + rows[0]) + frac_x * (rows[3] - 2.0 * rows[2] + rows[1])

    level, slope, bend = across(level), across(slope), across(bend)
    return tilt(level), flat(slope), curve(level), flat(bend), tilt(slope)


def trace_kernel(
    plane_ref, tile_ref, slot_ref, fine_ref, root_ref, own_ref, one_ref, two_ref, three_ref, offset_ref,
    disp_ref, dist_ref, patch_ref, coarse_ref
):
    planes = tile_ref.shape[0]
    for k, ref in enumerate((own_ref, one_ref, two_ref, three_ref)):
        coarse_ref[(plane_ref[0] + k) & (planes - 1)] = ref[...]
    slots = tile_ref.shape[1]
    rays = slot_ref.shape[1]
    step = 256

    def one(index, carry):
        plane = index // (rays // step)
        start = pl.multiple_of((index % (rays // step)) * step, step)
        slot = slot_ref[pl.ds(plane, 1), pl.ds(start, step)]
        cell = fine_ref[pl.ds(plane, 1), pl.ds(start, step)]
        ids = lax.broadcasted_iota(jnp.int32, (slots, step), 0)
        onehot = (ids == slot).astype(jnp.float32).astype(jnp.bfloat16)
        picked = lax.dot_general(
            tile_ref[plane], onehot, (((0,), (0,)), ((), ())), preferred_element_type=jnp.float32
        )
        off_x = cell % TP - 1
        off_y = cell // TP - 1
        low = shift_rows([picked[TP * y : TP * y + 8] for y in range(TP)], off_y, (8, 4, 2, 1), 4)
        high = shift_rows([picked[TP * y + 8 : TP * y + 16] for y in range(TP)], off_y, (8, 4, 2, 1), 4)
        for i in range(4):
            first = jnp.where(off_x >= 8, high[i], low[i])
            patch_ref[plane, i, :, pl.ds(start, step)] = shift_within(first, high[i], off_x)
        return carry

    lax.fori_loop(0, planes * (rays // step), one, 0)

    offset = [offset_ref[0:1], offset_ref[1:2]]
    disp = [jnp.zeros((1, rays), jnp.float32)] * 2
    last = disp
    zero = jnp.zeros((1, rays), jnp.float32)
    unit = jnp.ones((1, rays), jnp.float32)
    dist = [unit, zero, zero, unit]
    before = dist
    for plane in range(planes):
        chi = float(FIRST + plane)
        ahead = 2.0 * chi / (chi + 1.0)
        behind = (chi - 1.0) / (chi + 1.0)
        strength = chi / (chi + 1.0)
        position = [offset[0] + disp[0], offset[1] + disp[1]]
        fine = stencil_terms([patch_ref[plane, i] for i in range(4)], position[0], position[1])
        cell = fine_ref[plane : plane + 1]
        root = root_ref[plane : plane + 1]
        base_x = ((root % 2) * (RATIO // 2) + cell % TP).astype(jnp.float32)
        base_y = ((root // 2) * (RATIO // 2) + cell // TP).astype(jnp.float32)
        coarse = stencil_terms(
            [coarse_ref[plane, 4 * i : 4 * i + 4] for i in range(4)],
            (base_x + position[0]) * (1.0 / RATIO),
            (base_y + position[1]) * (1.0 / RATIO),
        )
        once = UNIT / RATIO
        twice = UNIT / (RATIO * RATIO)
        grad_x = fine[0] + coarse[0] * once
        grad_y = fine[1] + coarse[1] * once
        xx = fine[2] + coarse[2] * twice
        yy = fine[3] + coarse[3] * twice
        xy = fine[4] + coarse[4] * twice
        new_disp = [
            ahead * disp[0] - behind * last[0] - strength * grad_x,
            ahead * disp[1] - behind * last[1] - strength * grad_y,
        ]
        product = [
            xx * dist[0] + xy * dist[2],
            xx * dist[1] + xy * dist[3],
            xy * dist[0] + yy * dist[2],
            xy * dist[1] + yy * dist[3],
        ]
        new_dist = [ahead * dist[k] - behind * before[k] - strength * product[k] for k in range(4)]
        disp, last, dist, before = new_disp, disp, new_dist, dist
    for k in range(2):
        disp_ref[k : k + 1] = disp[k]
    for k in range(4):
        dist_ref[k : k + 1] = dist[k]


def swap(array, axes):
    return lax.all_to_all(array, axes, split_axis=0, concat_axis=0, tiled=True)


def body(
    coarse_potential,
    fine_tiles,
    tile_requests,
    ray_slot,
    fine_cell,
    coarse_cell,
    tile_root,
    ray_offset,
):
    planes = lax.axis_size("plane")
    owners = lax.axis_size("ray")
    slots = tile_requests.shape[3]
    side = coarse_potential.shape[1]
    rays = ray_offset.shape[1]
    cells = TP * TP
    vmem = pl.BlockSpec(memory_space=pltpu.VMEM)
    smem = pl.BlockSpec(memory_space=pltpu.SMEM)
    plane = jnp.full((1,), lax.axis_index("plane"), jnp.int32)

    def hop(array, by):
        return lax.ppermute(array, "plane", [(i, (i + by) % planes) for i in range(planes)])

    size = coarse_potential.shape[0] * side // 2 // LANES
    message = pl.pallas_call(
        pack_kernel,
        out_shape=jax.ShapeDtypeStruct((owners, size + 8, LANES), jnp.int32),
        in_specs=[vmem] * 2,
        out_specs=vmem,
        scratch_shapes=[pltpu.VMEM((owners, LANES), jnp.int32)],
        name="pack",
    )(coarse_potential, tile_requests.reshape(planes, owners, slots))
    messages = swap(message, "ray")
    cell_parts = [coarse_cell] + [hop(coarse_cell, k) for k in range(1, planes)]
    asked = messages[:, size]
    asked_parts = [asked] + [hop(asked, k) for k in range(1, planes)]

    outgoing = pl.pallas_call(
        take_kernel,
        out_shape=jax.ShapeDtypeStruct((planes, owners, slots, cells), jnp.bfloat16),
        in_specs=[smem] + [vmem] * 5,
        out_specs=vmem,
        scratch_shapes=[pltpu.VMEM((LANES, owners), jnp.int32)],
        compiler_params=pltpu.CompilerParams(vmem_limit_bytes=32 << 20),
        cost_estimate=pl.CostEstimate(flops=1_100_000_000, bytes_accessed=1_600_000, transcendentals=0),
        name="take",
    )(plane, *asked_parts, fine_tiles[0])
    arrived = swap(outgoing.reshape(planes * owners, slots, cells), ("plane", "ray"))

    found = pl.pallas_call(
        coarse_kernel,
        out_shape=jax.ShapeDtypeStruct((planes, 16, rays), jnp.float32),
        in_specs=[smem] + [vmem] * 5,
        out_specs=vmem,
        scratch_shapes=[
            pltpu.VMEM((2 * side // WIN * (side // LANES), (TALL + 1) * LANES), jnp.bfloat16),
            pltpu.VMEM((planes, rays), jnp.int32),
        ],
        compiler_params=pltpu.CompilerParams(vmem_limit_bytes=32 << 20),
        cost_estimate=pl.CostEstimate(flops=6_000_000_000, bytes_accessed=1_500_000, transcendentals=0),
        name="coarse",
    )(plane, messages, *cell_parts)
    found_parts = [found[0]] + [hop(found[k], planes - k) for k in range(1, planes)]

    return pl.pallas_call(
        trace_kernel,
        out_shape=(
            jax.ShapeDtypeStruct((2, rays), jnp.float32),
            jax.ShapeDtypeStruct((4, rays), jnp.float32),
        ),
        in_specs=[smem] + [vmem] * 9,
        out_specs=(vmem,) * 2,
        scratch_shapes=[
            pltpu.VMEM((planes, 4, 8, rays), jnp.float32),
            pltpu.VMEM((planes, 16, rays), jnp.float32),
        ],
        compiler_params=pltpu.CompilerParams(vmem_limit_bytes=32 << 20),
        cost_estimate=pl.CostEstimate(flops=1_500_000_000, bytes_accessed=1_500_000, transcendentals=0),
        name="trace",
    )(
        plane,
        arrived.reshape(planes, owners * slots, cells),
        ray_slot,
        fine_cell,
        tile_root,
        *found_parts,
        ray_offset,
    )


def solution(mesh):
    in_specs = (
        P(("plane", "ray"), None),
        P("plane", "ray", None),
        P(("plane", "ray"), None, None, None),
        P(None, ("plane", "ray")),
        P(None, ("plane", "ray")),
        P(None, ("plane", "ray")),
        P(None, ("plane", "ray")),
        P(None, ("plane", "ray")),
    )
    out_specs = (P(None, ("plane", "ray")), P(None, ("plane", "ray")))
    return jax.shard_map(body, mesh=mesh, in_specs=in_specs, out_specs=out_specs, check_vma=False)
```

```python
import jax
import jax.numpy as jnp
from jax import lax
from jax.experimental import pallas as pl
from jax.experimental.pallas import tpu as pltpu
from jax.sharding import PartitionSpec as P

TP = 16
RATIO = 32
FIRST = 31
LANES = 128
HALO = 8
WIN = 8
TALL = WIN + 3
UNIT = 72.0 / 32767.0


def shift_rows(rows, amount, bits, keep):
    left = sum(bits)
    for bit in bits:
        left -= bit
        taken = (amount & bit) != 0
        need = keep + left
        rows = [
            jnp.where(taken, rows[j + bit], rows[j]) if j + bit < len(rows) else rows[j]
            for j in range(min(need, len(rows)))
        ]
    return rows


def shift_within(low, high, amount):
    index = lax.broadcasted_iota(jnp.int32, low.shape, 0)
    far = jnp.where(index < 4, pltpu.roll(low, 4, 0), pltpu.roll(high, 4, 0))
    here = jnp.where((amount & 4) != 0, far, low)
    here = jnp.where((amount & 2) != 0, pltpu.roll(here, 6, 0), here)
    return jnp.where((amount & 1) != 0, pltpu.roll(here, 7, 0), here)


def pack_kernel(coarse_ref, request_ref, out_ref, row_ref):
    planes, owners, slots = request_ref.shape
    side = coarse_ref.shape[1]
    half = side // 2
    code = jnp.floor(coarse_ref[...] * (1.0 / UNIT) + 0.5).astype(jnp.int32)
    word = (code[:, :half] << 16) | (code[:, half:] & 0xFFFF)
    tiles = []
    for y in range(coarse_ref.shape[0] // WIN):
        for x in range(half // LANES):
            tiles.append(word[y * WIN : (y + 1) * WIN, x * LANES : (x + 1) * LANES])
    block = jnp.concatenate(tiles, axis=0)
    row_ref[...] = jnp.zeros_like(row_ref)
    for plane in range(planes):
        row_ref[:, plane * slots : (plane + 1) * slots] = request_ref[plane]
    size = block.shape[0]
    for owner in range(owners):
        out_ref[owner, 0:size] = block
        out_ref[owner, size : size + 8] = jnp.broadcast_to(row_ref[owner : owner + 1], (8, LANES))


def take_kernel(plane_ref, own_ref, one_ref, two_ref, three_ref, tile_ref, out_ref, turned_ref):
    planes, owners, slots, cells = out_ref.shape
    plane = plane_ref[0]
    count = tile_ref.shape[0]
    group = 16
    ids = lax.broadcasted_iota(jnp.int32, (slots, count), 1)
    for k, ref in enumerate((own_ref, one_ref, two_ref, three_ref)):
        turned_ref[...] = jnp.transpose(ref[...])
        wanted = turned_ref[pl.ds(pl.multiple_of(plane * slots, slots), slots), :]
        source = (plane + planes - k) & (planes - 1)
        for first in range(0, owners, group):
            onehot = jnp.concatenate(
                [(ids == wanted[:, r : r + 1]).astype(jnp.float32).astype(jnp.bfloat16) for r in range(first, first + group)],
                axis=0,
            )
            got = jnp.dot(onehot, tile_ref[...], preferred_element_type=jnp.float32).astype(jnp.bfloat16)
            out_ref[source, pl.ds(first, group)] = got.reshape(group, slots, cells)


def coarse_kernel(plane_ref, grid_ref, own_ref, one_ref, two_ref, three_ref, out_ref, table_ref, cell_ref):
    owners, rows, _ = grid_ref.shape
    plane = plane_ref[0]
    side = owners * 2 * WIN
    windows = side // WIN
    chunks = side // LANES
    halves = chunks // 2
    width = TALL * LANES
    step = 256
    count = windows * chunks
    grid = grid_ref.reshape(owners * rows, LANES)

    def load(chunk, dy):
        parts = []
        for parity in range(2):
            pick = (parity + dy // WIN) % 2
            start = (pick * halves + chunk % halves) * WIN + dy % WIN
            part = grid[pl.ds(start, owners, stride=rows), :]
            if parity + dy // WIN >= 2:
                part = pltpu.roll(part, owners - 1, 0)
            parts.append(part)
        word = jnp.concatenate(parts, axis=0)
        return word >> 16 if chunk < halves else (word << 16) >> 16

    def put(code, start, column):
        high = ((code + 128) >> 8) << 8
        table_ref[pl.ds(start, windows), pl.ds(column, LANES)] = high.astype(jnp.float32).astype(jnp.bfloat16)
        table_ref[pl.ds(count + start, windows), pl.ds(column, LANES)] = (
            (code - high).astype(jnp.float32).astype(jnp.bfloat16)
        )

    lane = lax.broadcasted_iota(jnp.int32, (windows, LANES), 1)
    for chunk in range(chunks):
        base = chunk * windows
        halo = jnp.zeros((windows, LANES), jnp.int32)
        for dy in range(TALL):
            near = load((chunk + 1) % chunks, dy)
            near = pltpu.roll(near, dy * HALO, 1) if dy else near
            halo = jnp.where((lane >= dy * HALO) & (lane < (dy + 1) * HALO), near, halo)
            put(load(chunk, dy), base, dy * LANES)
        put(halo, base, width)

    for k, ref in enumerate((own_ref, one_ref, two_ref, three_ref)):
        cell_ref[k : k + 1] = ref[pl.ds(plane, 1), :]

    bundles = cell_ref.shape[0]
    per = cell_ref.shape[1] // step

    def one(index, carry):
        bundle = index // per
        start = pl.multiple_of((index % per) * step, step)
        cell = cell_ref[pl.ds(bundle, 1), pl.ds(start, step)]
        first_x = (cell - 1) & (side - 1)
        first_y = (cell // side - 1) & (side - 1)
        tall = first_y // WIN
        window = (first_x // LANES) * windows + (tall & 1) * owners + tall // 2
        ids = lax.broadcasted_iota(jnp.int32, (count, step), 0)
        onehot = (ids == window).astype(jnp.float32).astype(jnp.bfloat16)
        onehot = jnp.concatenate([onehot, onehot], axis=0)
        picked = lax.dot_general(
            table_ref[...], onehot, (((0,), (0,)), ((), ())), preferred_element_type=jnp.float32
        )
        off_y = first_y & (WIN - 1)
        off_x = first_x & (LANES - 1)
        lines = []
        for dy in range(TALL):
            parts = [picked[dy * LANES + 8 * k : dy * LANES + 8 * k + 8] for k in range(LANES // 8)]
            parts.append(picked[width + dy * HALO : width + (dy + 1) * HALO])
            lines.append(shift_rows(parts, off_x // 8, (8, 4, 2, 1), 2))
        low = shift_rows([line[0] for line in lines], off_y, (4, 2, 1), 4)
        high = shift_rows([line[1] for line in lines], off_y, (4, 2, 1), 4)
        patch = [shift_within(low[i], high[i], off_x)[:4] for i in range(4)]
        out_ref[bundle, :, pl.ds(start, step)] = jnp.concatenate(patch, axis=0)
        return carry

    lax.fori_loop(0, bundles * per, one, 0)


def stencil_terms(patch, frac_x, frac_y):
    keep_y = 1.0 - frac_y
    level = keep_y * patch[1] + frac_y * patch[2]
    slope = (keep_y * (patch[2] - patch[0]) + frac_y * (patch[3] - patch[1])) * 0.5
    bend = keep_y * (patch[2] - 2.0 * patch[1] + patch[0]) + frac_y * (patch[3] - 2.0 * patch[2] + patch[1])
    keep_x = 1.0 - frac_x

    def across(rows):
        return [rows[k : k + 1] for k in range(4)]

    def flat(rows):
        return keep_x * rows[1] + frac_x * rows[2]

    def tilt(rows):
        return (keep_x * (rows[2] - rows[0]) + frac_x * (rows[3] - rows[1])) * 0.5

    def curve(rows):
        return keep_x * (rows[2] - 2.0 * rows[1] + rows[0]) + frac_x * (rows[3] - 2.0 * rows[2] + rows[1])

    level, slope, bend = across(level), across(slope), across(bend)
    return tilt(level), flat(slope), curve(level), flat(bend), tilt(slope)


def trace_kernel(
    plane_ref, tile_ref, slot_ref, fine_ref, root_ref, own_ref, one_ref, two_ref, three_ref, offset_ref,
    disp_ref, dist_ref, patch_ref, coarse_ref
):
    planes = tile_ref.shape[0]
    for k, ref in enumerate((own_ref, one_ref, two_ref, three_ref)):
        coarse_ref[(plane_ref[0] + k) & (planes - 1)] = ref[...]
    slots = tile_ref.shape[1]
    rays = slot_ref.shape[1]
    step = 256

    def one(index, carry):
        plane = index // (rays // step)
        start = pl.multiple_of((index % (rays // step)) * step, step)
        slot = slot_ref[pl.ds(plane, 1), pl.ds(start, step)]
        cell = fine_ref[pl.ds(plane, 1), pl.ds(start, step)]
        ids = lax.broadcasted_iota(jnp.int32, (slots, step), 0)
        onehot = (ids == slot).astype(jnp.float32).astype(jnp.bfloat16)
        picked = lax.dot_general(
            tile_ref[plane], onehot, (((0,), (0,)), ((), ())), preferred_element_type=jnp.float32
        )
        off_x = cell % TP - 1
        off_y = cell // TP - 1
        low = shift_rows([picked[TP * y : TP * y + 8] for y in range(TP)], off_y, (8, 4, 2, 1), 4)
        high = shift_rows([picked[TP * y + 8 : TP * y + 16] for y in range(TP)], off_y, (8, 4, 2, 1), 4)
        for i in range(4):
            first = jnp.where(off_x >= 8, high[i], low[i])
            patch_ref[plane, i, :, pl.ds(start, step)] = shift_within(first, high[i], off_x)
        return carry

    lax.fori_loop(0, planes * (rays // step), one, 0)

    offset = [offset_ref[0:1], offset_ref[1:2]]
    disp = [jnp.zeros((1, rays), jnp.float32)] * 2
    last = disp
    zero = jnp.zeros((1, rays), jnp.float32)
    unit = jnp.ones((1, rays), jnp.float32)
    dist = [unit, zero, zero, unit]
    before = dist
    for plane in range(planes):
        chi = float(FIRST + plane)
        ahead = 2.0 * chi / (chi + 1.0)
        behind = (chi - 1.0) / (chi + 1.0)
        strength = chi / (chi + 1.0)
        position = [offset[0] + disp[0], offset[1] + disp[1]]
        fine = stencil_terms([patch_ref[plane, i] for i in range(4)], position[0], position[1])
        cell = fine_ref[plane : plane + 1]
        root = root_ref[plane : plane + 1]
        base_x = ((root % 2) * (RATIO // 2) + cell % TP).astype(jnp.float32)
        base_y = ((root // 2) * (RATIO // 2) + cell // TP).astype(jnp.float32)
        coarse = stencil_terms(
            [coarse_ref[plane, 4 * i : 4 * i + 4] for i in range(4)],
            (base_x + position[0]) * (1.0 / RATIO),
            (base_y + position[1]) * (1.0 / RATIO),
        )
        once = UNIT / RATIO
        twice = UNIT / (RATIO * RATIO)
        grad_x = fine[0] + coarse[0] * once
        grad_y = fine[1] + coarse[1] * once
        xx = fine[2] + coarse[2] * twice
        yy = fine[3] + coarse[3] * twice
        xy = fine[4] + coarse[4] * twice
        new_disp = [
            ahead * disp[0] - behind * last[0] - strength * grad_x,
            ahead * disp[1] - behind * last[1] - strength * grad_y,
        ]
        product = [
            xx * dist[0] + xy * dist[2],
            xx * dist[1] + xy * dist[3],
            xy * dist[0] + yy * dist[2],
            xy * dist[1] + yy * dist[3],
        ]
        new_dist = [ahead * dist[k] - behind * before[k] - strength * product[k] for k in range(4)]
        disp, last, dist, before = new_disp, disp, new_dist, dist
    for k in range(2):
        disp_ref[k : k + 1] = disp[k]
    for k in range(4):
        dist_ref[k : k + 1] = dist[k]


def swap(array, axes):
    return lax.all_to_all(array, axes, split_axis=0, concat_axis=0, tiled=True)


def body(
    coarse_potential,
    fine_tiles,
    tile_requests,
    ray_slot,
    fine_cell,
    coarse_cell,
    tile_root,
    ray_offset,
):
    planes = lax.axis_size("plane")
    owners = lax.axis_size("ray")
    slots = tile_requests.shape[3]
    side = coarse_potential.shape[1]
    rays = ray_offset.shape[1]
    cells = TP * TP
    vmem = pl.BlockSpec(memory_space=pltpu.VMEM)
    smem = pl.BlockSpec(memory_space=pltpu.SMEM)
    plane = jnp.full((1,), lax.axis_index("plane"), jnp.int32)

    def hop(array, by):
        return lax.ppermute(array, "plane", [(i, (i + by) % planes) for i in range(planes)])

    size = coarse_potential.shape[0] * side // 2 // LANES
    message = pl.pallas_call(
        pack_kernel,
        out_shape=jax.ShapeDtypeStruct((owners, size + 8, LANES), jnp.int32),
        in_specs=[vmem] * 2,
        out_specs=vmem,
        scratch_shapes=[pltpu.VMEM((owners, LANES), jnp.int32)],
        name="pack",
    )(coarse_potential, tile_requests.reshape(planes, owners, slots))
    messages = swap(message, "ray")
    cell_parts = [coarse_cell] + [hop(coarse_cell, k) for k in range(1, planes)]
    asked, *cell_parts = lax.optimization_barrier((messages[:, size], *cell_parts))
    asked_parts = [asked] + [hop(asked, k) for k in range(1, planes)]

    outgoing = pl.pallas_call(
        take_kernel,
        out_shape=jax.ShapeDtypeStruct((planes, owners, slots, cells), jnp.bfloat16),
        in_specs=[smem] + [vmem] * 5,
        out_specs=vmem,
        scratch_shapes=[pltpu.VMEM((LANES, owners), jnp.int32)],
        compiler_params=pltpu.CompilerParams(vmem_limit_bytes=32 << 20),
        cost_estimate=pl.CostEstimate(flops=1_100_000_000, bytes_accessed=1_600_000, transcendentals=0),
        name="take",
    )(plane, *asked_parts, fine_tiles[0])
    arrived = swap(outgoing.reshape(planes * owners, slots, cells), ("plane", "ray"))

    found = pl.pallas_call(
        coarse_kernel,
        out_shape=jax.ShapeDtypeStruct((planes, 16, rays), jnp.float32),
        in_specs=[smem] + [vmem] * 5,
        out_specs=vmem,
        scratch_shapes=[
            pltpu.VMEM((2 * side // WIN * (side // LANES), (TALL + 1) * LANES), jnp.bfloat16),
            pltpu.VMEM((planes, rays), jnp.int32),
        ],
        compiler_params=pltpu.CompilerParams(vmem_limit_bytes=32 << 20),
        cost_estimate=pl.CostEstimate(flops=6_000_000_000, bytes_accessed=1_500_000, transcendentals=0),
        name="coarse",
    )(plane, messages, *cell_parts)
    found_parts = [found[0]] + [hop(found[k], planes - k) for k in range(1, planes)]

    return pl.pallas_call(
        trace_kernel,
        out_shape=(
            jax.ShapeDtypeStruct((2, rays), jnp.float32),
            jax.ShapeDtypeStruct((4, rays), jnp.float32),
        ),
        in_specs=[smem] + [vmem] * 9,
        out_specs=(vmem,) * 2,
        scratch_shapes=[
            pltpu.VMEM((planes, 4, 8, rays), jnp.float32),
            pltpu.VMEM((planes, 16, rays), jnp.float32),
        ],
        compiler_params=pltpu.CompilerParams(vmem_limit_bytes=32 << 20),
        cost_estimate=pl.CostEstimate(flops=1_500_000_000, bytes_accessed=1_500_000, transcendentals=0),
        name="trace",
    )(
        plane,
        arrived.reshape(planes, owners * slots, cells),
        ray_slot,
        fine_cell,
        tile_root,
        *found_parts,
        ray_offset,
    )


def solution(mesh):
    in_specs = (
        P(("plane", "ray"), None),
        P("plane", "ray", None),
        P(("plane", "ray"), None, None, None),
        P(None, ("plane", "ray")),
        P(None, ("plane", "ray")),
        P(None, ("plane", "ray")),
        P(None, ("plane", "ray")),
        P(None, ("plane", "ray")),
    )
    out_specs = (P(None, ("plane", "ray")), P(None, ("plane", "ray")))
    return jax.shard_map(body, mesh=mesh, in_specs=in_specs, out_specs=out_specs, check_vma=False)
```

```python
import jax
import jax.numpy as jnp
from jax import lax
from jax.experimental import pallas as pl
from jax.experimental.pallas import tpu as pltpu
from jax.sharding import PartitionSpec as P

TP = 16
RATIO = 32
FIRST = 31
PLANES = 4
LANES = 128
HALO = 8
WIN = 8
TALL = WIN + 3
UNIT = 72.0 / 32767.0


def shift_rows(rows, amount, bits, keep):
    left = sum(bits)
    for bit in bits:
        left -= bit
        taken = (amount & bit) != 0
        need = keep + left
        rows = [
            jnp.where(taken, rows[j + bit], rows[j]) if j + bit < len(rows) else rows[j]
            for j in range(min(need, len(rows)))
        ]
    return rows


def shift_within(low, high, amount):
    index = lax.broadcasted_iota(jnp.int32, low.shape, 0)
    far = jnp.where(index < 4, pltpu.roll(low, 4, 0), pltpu.roll(high, 4, 0))
    here = jnp.where((amount & 4) != 0, far, low)
    here = jnp.where((amount & 2) != 0, pltpu.roll(here, 6, 0), here)
    return jnp.where((amount & 1) != 0, pltpu.roll(here, 7, 0), here)


def pack_kernel(plane_ref, coarse_ref, own_ref, one_ref, two_ref, three_ref, out_ref, wish_ref, row_ref):
    owners, rows, _ = out_ref.shape
    planes = PLANES
    slots = own_ref.shape[0] // planes
    side = coarse_ref.shape[1]
    half = side // 2
    code = jnp.floor(coarse_ref[...] * (1.0 / UNIT) + 0.5).astype(jnp.int32)
    word = (code[:, :half] << 16) | (code[:, half:] & 0xFFFF)
    tiles = []
    for y in range(coarse_ref.shape[0] // WIN):
        for x in range(half // LANES):
            tiles.append(word[y * WIN : (y + 1) * WIN, x * LANES : (x + 1) * LANES])
    block = jnp.concatenate(tiles, axis=0)
    plane = plane_ref[0]
    wish_ref[...] = jnp.zeros_like(wish_ref)
    for k, ref in enumerate((own_ref, one_ref, two_ref, three_ref)):
        source = (plane + planes - k) & (planes - 1)
        wish_ref[pl.ds(pl.multiple_of(source * slots, slots), slots), 0:owners] = ref[
            pl.ds(pl.multiple_of(plane * slots, slots), slots), :
        ]
    row_ref[...] = jnp.transpose(wish_ref[...])
    size = rows - 8
    for owner in range(owners):
        out_ref[owner, 0:size] = block
        out_ref[owner, size:rows] = jnp.broadcast_to(row_ref[owner : owner + 1], (8, LANES))


def take_kernel(asked_ref, tile_ref, out_ref, turned_ref):
    planes, owners, slots, cells = out_ref.shape
    count = tile_ref.shape[0]
    lot = planes * slots
    group = 4
    turned_ref[...] = jnp.transpose(asked_ref[...])
    ids = lax.broadcasted_iota(jnp.int32, (lot, count), 1)
    for first in range(0, owners, group):
        onehot = jnp.concatenate(
            [
                (ids == turned_ref[0:lot, r : r + 1]).astype(jnp.float32).astype(jnp.bfloat16)
                for r in range(first, first + group)
            ],
            axis=0,
        )
        got = jnp.dot(onehot, tile_ref[...], preferred_element_type=jnp.float32).astype(jnp.bfloat16)
        for r in range(group):
            for p in range(planes):
                start = r * lot + p * slots
                out_ref[p, first + r] = got[start : start + slots]


def coarse_kernel(plane_ref, grid_ref, own_ref, one_ref, two_ref, three_ref, out_ref, table_ref, cell_ref):
    owners, rows, _ = grid_ref.shape
    plane = plane_ref[0]
    side = owners * 2 * WIN
    windows = side // WIN
    chunks = side // LANES
    halves = chunks // 2
    width = TALL * LANES
    step = 256
    count = windows * chunks
    grid = grid_ref.reshape(owners * rows, LANES)

    def load(chunk, dy):
        parts = []
        for parity in range(2):
            pick = (parity + dy // WIN) % 2
            start = (pick * halves + chunk % halves) * WIN + dy % WIN
            part = grid[pl.ds(start, owners, stride=rows), :]
            if parity + dy // WIN >= 2:
                part = pltpu.roll(part, owners - 1, 0)
            parts.append(part)
        word = jnp.concatenate(parts, axis=0)
        return word >> 16 if chunk < halves else (word << 16) >> 16

    def put(code, start, column):
        high = ((code + 128) >> 8) << 8
        table_ref[pl.ds(start, windows), pl.ds(column, LANES)] = high.astype(jnp.float32).astype(jnp.bfloat16)
        table_ref[pl.ds(count + start, windows), pl.ds(column, LANES)] = (
            (code - high).astype(jnp.float32).astype(jnp.bfloat16)
        )

    lane = lax.broadcasted_iota(jnp.int32, (windows, LANES), 1)
    for chunk in range(chunks):
        base = chunk * windows
        halo = jnp.zeros((windows, LANES), jnp.int32)
        for dy in range(TALL):
            near = load((chunk + 1) % chunks, dy)
            near = pltpu.roll(near, dy * HALO, 1) if dy else near
            halo = jnp.where((lane >= dy * HALO) & (lane < (dy + 1) * HALO), near, halo)
            put(load(chunk, dy), base, dy * LANES)
        put(halo, base, width)

    for k, ref in enumerate((own_ref, one_ref, two_ref, three_ref)):
        cell_ref[k : k + 1] = ref[pl.ds(plane, 1), :]

    bundles = cell_ref.shape[0]
    per = cell_ref.shape[1] // step

    def one(index, carry):
        bundle = index // per
        start = pl.multiple_of((index % per) * step, step)
        cell = cell_ref[pl.ds(bundle, 1), pl.ds(start, step)]
        first_x = (cell - 1) & (side - 1)
        first_y = (cell // side - 1) & (side - 1)
        tall = first_y // WIN
        window = (first_x // LANES) * windows + (tall & 1) * owners + tall // 2
        ids = lax.broadcasted_iota(jnp.int32, (count, step), 0)
        onehot = (ids == window).astype(jnp.float32).astype(jnp.bfloat16)
        onehot = jnp.concatenate([onehot, onehot], axis=0)
        picked = lax.dot_general(
            table_ref[...], onehot, (((0,), (0,)), ((), ())), preferred_element_type=jnp.float32
        )
        off_y = first_y & (WIN - 1)
        off_x = first_x & (LANES - 1)
        lines = []
        for dy in range(TALL):
            parts = [picked[dy * LANES + 8 * k : dy * LANES + 8 * k + 8] for k in range(LANES // 8)]
            parts.append(picked[width + dy * HALO : width + (dy + 1) * HALO])
            lines.append(shift_rows(parts, off_x // 8, (8, 4, 2, 1), 2))
        low = shift_rows([line[0] for line in lines], off_y, (4, 2, 1), 4)
        high = shift_rows([line[1] for line in lines], off_y, (4, 2, 1), 4)
        patch = [shift_within(low[i], high[i], off_x)[:4] for i in range(4)]
        out_ref[bundle, :, pl.ds(start, step)] = jnp.concatenate(patch, axis=0)
        return carry

    lax.fori_loop(0, bundles * per, one, 0)


def stencil_terms(patch, frac_x, frac_y):
    keep_y = 1.0 - frac_y
    level = keep_y * patch[1] + frac_y * patch[2]
    slope = (keep_y * (patch[2] - patch[0]) + frac_y * (patch[3] - patch[1])) * 0.5
    bend = keep_y * (patch[2] - 2.0 * patch[1] + patch[0]) + frac_y * (patch[3] - 2.0 * patch[2] + patch[1])
    keep_x = 1.0 - frac_x

    def across(rows):
        return [rows[k : k + 1] for k in range(4)]

    def flat(rows):
        return keep_x * rows[1] + frac_x * rows[2]

    def tilt(rows):
        return (keep_x * (rows[2] - rows[0]) + frac_x * (rows[3] - rows[1])) * 0.5

    def curve(rows):
        return keep_x * (rows[2] - 2.0 * rows[1] + rows[0]) + frac_x * (rows[3] - 2.0 * rows[2] + rows[1])

    level, slope, bend = across(level), across(slope), across(bend)
    return tilt(level), flat(slope), curve(level), flat(bend), tilt(slope)


def trace_kernel(
    plane_ref, tile_ref, slot_ref, fine_ref, root_ref, own_ref, one_ref, two_ref, three_ref, offset_ref,
    disp_ref, dist_ref, patch_ref, coarse_ref
):
    planes = tile_ref.shape[0]
    for k, ref in enumerate((own_ref, one_ref, two_ref, three_ref)):
        coarse_ref[(plane_ref[0] + k) & (planes - 1)] = ref[...]
    slots = tile_ref.shape[1]
    rays = slot_ref.shape[1]
    step = 256

    def one(index, carry):
        plane = index // (rays // step)
        start = pl.multiple_of((index % (rays // step)) * step, step)
        slot = slot_ref[pl.ds(plane, 1), pl.ds(start, step)]
        cell = fine_ref[pl.ds(plane, 1), pl.ds(start, step)]
        ids = lax.broadcasted_iota(jnp.int32, (slots, step), 0)
        onehot = (ids == slot).astype(jnp.float32).astype(jnp.bfloat16)
        picked = lax.dot_general(
            tile_ref[plane], onehot, (((0,), (0,)), ((), ())), preferred_element_type=jnp.float32
        )
        off_x = cell % TP - 1
        off_y = cell // TP - 1
        low = shift_rows([picked[TP * y : TP * y + 8] for y in range(TP)], off_y, (8, 4, 2, 1), 4)
        high = shift_rows([picked[TP * y + 8 : TP * y + 16] for y in range(TP)], off_y, (8, 4, 2, 1), 4)
        for i in range(4):
            first = jnp.where(off_x >= 8, high[i], low[i])
            patch_ref[plane, i, :, pl.ds(start, step)] = shift_within(first, high[i], off_x)
        return carry

    lax.fori_loop(0, planes * (rays // step), one, 0)

    offset = [offset_ref[0:1], offset_ref[1:2]]
    disp = [jnp.zeros((1, rays), jnp.float32)] * 2
    last = disp
    zero = jnp.zeros((1, rays), jnp.float32)
    unit = jnp.ones((1, rays), jnp.float32)
    dist = [unit, zero, zero, unit]
    before = dist
    for plane in range(planes):
        chi = float(FIRST + plane)
        ahead = 2.0 * chi / (chi + 1.0)
        behind = (chi - 1.0) / (chi + 1.0)
        strength = chi / (chi + 1.0)
        position = [offset[0] + disp[0], offset[1] + disp[1]]
        fine = stencil_terms([patch_ref[plane, i] for i in range(4)], position[0], position[1])
        cell = fine_ref[plane : plane + 1]
        root = root_ref[plane : plane + 1]
        base_x = ((root % 2) * (RATIO // 2) + cell % TP).astype(jnp.float32)
        base_y = ((root // 2) * (RATIO // 2) + cell // TP).astype(jnp.float32)
        coarse = stencil_terms(
            [coarse_ref[plane, 4 * i : 4 * i + 4] for i in range(4)],
            (base_x + position[0]) * (1.0 / RATIO),
            (base_y + position[1]) * (1.0 / RATIO),
        )
        once = UNIT / RATIO
        twice = UNIT / (RATIO * RATIO)
        grad_x = fine[0] + coarse[0] * once
        grad_y = fine[1] + coarse[1] * once
        xx = fine[2] + coarse[2] * twice
        yy = fine[3] + coarse[3] * twice
        xy = fine[4] + coarse[4] * twice
        new_disp = [
            ahead * disp[0] - behind * last[0] - strength * grad_x,
            ahead * disp[1] - behind * last[1] - strength * grad_y,
        ]
        product = [
            xx * dist[0] + xy * dist[2],
            xx * dist[1] + xy * dist[3],
            xy * dist[0] + yy * dist[2],
            xy * dist[1] + yy * dist[3],
        ]
        new_dist = [ahead * dist[k] - behind * before[k] - strength * product[k] for k in range(4)]
        disp, last, dist, before = new_disp, disp, new_dist, dist
    for k in range(2):
        disp_ref[k : k + 1] = disp[k]
    for k in range(4):
        dist_ref[k : k + 1] = dist[k]


def swap(array, axes):
    return lax.all_to_all(array, axes, split_axis=0, concat_axis=0, tiled=True)


def body(
    coarse_potential,
    fine_tiles,
    tile_requests,
    ray_slot,
    fine_cell,
    coarse_cell,
    tile_root,
    ray_offset,
):
    planes = lax.axis_size("plane")
    owners = lax.axis_size("ray")
    slots = tile_requests.shape[3]
    side = coarse_potential.shape[1]
    rays = ray_offset.shape[1]
    cells = TP * TP
    vmem = pl.BlockSpec(memory_space=pltpu.VMEM)
    smem = pl.BlockSpec(memory_space=pltpu.SMEM)
    plane = jnp.full((1,), lax.axis_index("plane"), jnp.int32)

    def hop(array, by):
        return lax.ppermute(array, "plane", [(i, (i + by) % planes) for i in range(planes)])

    wishes = tile_requests[0].transpose(0, 2, 1).reshape(planes * slots, owners)
    wish_parts = [wishes] + [hop(wishes, k) for k in range(1, planes)]
    coarse_cell, *wish_parts = lax.optimization_barrier((coarse_cell, *wish_parts))
    size = coarse_potential.shape[0] * side // 2 // LANES
    message = pl.pallas_call(
        pack_kernel,
        out_shape=jax.ShapeDtypeStruct((owners, size + 8, LANES), jnp.int32),
        in_specs=[smem] + [vmem] * 5,
        out_specs=vmem,
        scratch_shapes=[pltpu.VMEM((LANES, LANES), jnp.int32)] * 2,
        name="pack",
    )(plane, coarse_potential, *wish_parts)
    messages = swap(message, "ray")
    cell_parts = [coarse_cell] + [hop(coarse_cell, k) for k in range(1, planes)]
    asked, *cell_parts = lax.optimization_barrier((messages[:, size], *cell_parts))

    outgoing = pl.pallas_call(
        take_kernel,
        out_shape=jax.ShapeDtypeStruct((planes, owners, slots, cells), jnp.bfloat16),
        in_specs=[vmem] * 2,
        out_specs=vmem,
        scratch_shapes=[pltpu.VMEM((LANES, owners), jnp.int32)],
        compiler_params=pltpu.CompilerParams(vmem_limit_bytes=32 << 20),
        cost_estimate=pl.CostEstimate(flops=1_100_000_000, bytes_accessed=1_600_000, transcendentals=0),
        name="take",
    )(asked, fine_tiles[0])
    arrived = swap(outgoing.reshape(planes * owners, slots, cells), ("plane", "ray"))

    found = pl.pallas_call(
        coarse_kernel,
        out_shape=jax.ShapeDtypeStruct((planes, 16, rays), jnp.float32),
        in_specs=[smem] + [vmem] * 5,
        out_specs=vmem,
        scratch_shapes=[
            pltpu.VMEM((2 * side // WIN * (side // LANES), (TALL + 1) * LANES), jnp.bfloat16),
            pltpu.VMEM((planes, rays), jnp.int32),
        ],
        compiler_params=pltpu.CompilerParams(vmem_limit_bytes=32 << 20),
        cost_estimate=pl.CostEstimate(flops=6_000_000_000, bytes_accessed=1_500_000, transcendentals=0),
        name="coarse",
    )(plane, messages, *cell_parts)
    found_parts = [found[0]] + [hop(found[k], planes - k) for k in range(1, planes)]

    return pl.pallas_call(
        trace_kernel,
        out_shape=(
            jax.ShapeDtypeStruct((2, rays), jnp.float32),
            jax.ShapeDtypeStruct((4, rays), jnp.float32),
        ),
        in_specs=[smem] + [vmem] * 9,
        out_specs=(vmem,) * 2,
        scratch_shapes=[
            pltpu.VMEM((planes, 4, 8, rays), jnp.float32),
            pltpu.VMEM((planes, 16, rays), jnp.float32),
        ],
        compiler_params=pltpu.CompilerParams(vmem_limit_bytes=32 << 20),
        cost_estimate=pl.CostEstimate(flops=1_500_000_000, bytes_accessed=1_500_000, transcendentals=0),
        name="trace",
    )(
        plane,
        arrived.reshape(planes, owners * slots, cells),
        ray_slot,
        fine_cell,
        tile_root,
        *found_parts,
        ray_offset,
    )


def solution(mesh):
    in_specs = (
        P(("plane", "ray"), None),
        P("plane", "ray", None),
        P(("plane", "ray"), None, None, None),
        P(None, ("plane", "ray")),
        P(None, ("plane", "ray")),
        P(None, ("plane", "ray")),
        P(None, ("plane", "ray")),
        P(None, ("plane", "ray")),
    )
    out_specs = (P(None, ("plane", "ray")), P(None, ("plane", "ray")))
    return jax.shard_map(body, mesh=mesh, in_specs=in_specs, out_specs=out_specs, check_vma=False)
```

```python
import jax
import jax.numpy as jnp
from jax import lax
from jax.experimental import pallas as pl
from jax.experimental.pallas import tpu as pltpu
from jax.sharding import PartitionSpec as P

TP = 16
RATIO = 32
FIRST = 31
PLANES = 4
LANES = 128
HALO = 8
WIN = 8
TALL = WIN + 3
UNIT = 72.0 / 32767.0


def shift_rows(rows, amount, bits, keep):
    left = sum(bits)
    for bit in bits:
        left -= bit
        taken = (amount & bit) != 0
        need = keep + left
        rows = [
            jnp.where(taken, rows[j + bit], rows[j]) if j + bit < len(rows) else rows[j]
            for j in range(min(need, len(rows)))
        ]
    return rows


def shift_within(low, high, amount):
    index = lax.broadcasted_iota(jnp.int32, low.shape, 0)
    far = jnp.where(index < 4, pltpu.roll(low, 4, 0), pltpu.roll(high, 4, 0))
    here = jnp.where((amount & 4) != 0, far, low)
    here = jnp.where((amount & 2) != 0, pltpu.roll(here, 6, 0), here)
    return jnp.where((amount & 1) != 0, pltpu.roll(here, 7, 0), here)


def pack_kernel(plane_ref, coarse_ref, own_ref, one_ref, two_ref, three_ref, out_ref, wish_ref, row_ref):
    owners, rows, _ = out_ref.shape
    planes = PLANES
    slots = own_ref.shape[0] // planes
    side = coarse_ref.shape[1]
    half = side // 2
    code = jnp.floor(coarse_ref[...] * (1.0 / UNIT) + 0.5).astype(jnp.int32)
    word = (code[:, :half] << 16) | (code[:, half:] & 0xFFFF)
    tiles = []
    for y in range(coarse_ref.shape[0] // WIN):
        for x in range(half // LANES):
            tiles.append(word[y * WIN : (y + 1) * WIN, x * LANES : (x + 1) * LANES])
    block = jnp.concatenate(tiles, axis=0)
    plane = plane_ref[0]
    wish_ref[...] = jnp.zeros_like(wish_ref)
    for k, ref in enumerate((own_ref, one_ref, two_ref, three_ref)):
        source = (plane + planes - k) & (planes - 1)
        wish_ref[pl.ds(pl.multiple_of(source * slots, slots), slots), 0:owners] = ref[
            pl.ds(pl.multiple_of(plane * slots, slots), slots), :
        ]
    row_ref[...] = jnp.transpose(wish_ref[...])
    size = rows - 8
    for owner in range(owners):
        out_ref[owner, 0:size] = block
        out_ref[owner, size:rows] = jnp.broadcast_to(row_ref[owner : owner + 1], (8, LANES))


def take_kernel(asked_ref, tile_ref, out_ref, turned_ref):
    planes, owners, slots, cells = out_ref.shape
    count = tile_ref.shape[0]
    lot = planes * slots
    group = 4
    turned_ref[...] = jnp.transpose(asked_ref[...])
    ids = lax.broadcasted_iota(jnp.int32, (lot, count), 1)
    for first in range(0, owners, group):
        onehot = jnp.concatenate(
            [
                (ids == turned_ref[0:lot, r : r + 1]).astype(jnp.float32).astype(jnp.bfloat16)
                for r in range(first, first + group)
            ],
            axis=0,
        )
        got = jnp.dot(onehot, tile_ref[...], preferred_element_type=jnp.float32).astype(jnp.bfloat16)
        for r in range(group):
            for p in range(planes):
                start = r * lot + p * slots
                out_ref[p, first + r] = got[start : start + slots]


def coarse_kernel(
    plane_ref, grid_ref, own_ref, one_ref, two_ref, three_ref, out_ref,
    table_ref, cell_ref, hot_a, hot_b, picked_a, picked_b
):
    owners, rows, _ = grid_ref.shape
    plane = plane_ref[0]
    side = owners * 2 * WIN
    windows = side // WIN
    chunks = side // LANES
    halves = chunks // 2
    width = TALL * LANES
    step = picked_a.shape[1]
    count = windows * chunks
    grid = grid_ref.reshape(owners * rows, LANES)

    def load(chunk, dy):
        parts = []
        for parity in range(2):
            pick = (parity + dy // WIN) % 2
            start = (pick * halves + chunk % halves) * WIN + dy % WIN
            part = grid[pl.ds(start, owners, stride=rows), :]
            if parity + dy // WIN >= 2:
                part = pltpu.roll(part, owners - 1, 0)
            parts.append(part)
        word = jnp.concatenate(parts, axis=0)
        return word >> 16 if chunk < halves else (word << 16) >> 16

    def put(code, start, column):
        high = ((code + 128) >> 8) << 8
        table_ref[pl.ds(start, windows), pl.ds(column, LANES)] = high.astype(jnp.float32).astype(jnp.bfloat16)
        table_ref[pl.ds(count + start, windows), pl.ds(column, LANES)] = (
            (code - high).astype(jnp.float32).astype(jnp.bfloat16)
        )

    lane = lax.broadcasted_iota(jnp.int32, (windows, LANES), 1)
    for chunk in range(chunks):
        base = chunk * windows
        halo = jnp.zeros((windows, LANES), jnp.int32)
        for dy in range(TALL):
            near = load((chunk + 1) % chunks, dy)
            near = pltpu.roll(near, dy * HALO, 1) if dy else near
            halo = jnp.where((lane >= dy * HALO) & (lane < (dy + 1) * HALO), near, halo)
            put(load(chunk, dy), base, dy * LANES)
        put(halo, base, width)

    for k, ref in enumerate((own_ref, one_ref, two_ref, three_ref)):
        cell_ref[k : k + 1] = ref[pl.ds(plane, 1), :]

    bundles = cell_ref.shape[0]
    per = cell_ref.shape[1] // step

    def cells_of(index):
        bundle = index // per
        start = pl.multiple_of((index % per) * step, step)
        cell = cell_ref[pl.ds(bundle, 1), pl.ds(start, step)]
        return bundle, start, (cell - 1) & (side - 1), (cell // side - 1) & (side - 1)

    def select(index, hot_ref):
        _, _, first_x, first_y = cells_of(index)
        tall = first_y // WIN
        window = (first_x // LANES) * windows + (tall & 1) * owners + tall // 2
        ids = lax.broadcasted_iota(jnp.int32, (count, step), 0)
        onehot = (ids == window).astype(jnp.float32).astype(jnp.bfloat16)
        hot_ref[0:count] = onehot
        hot_ref[count : 2 * count] = onehot

    def pick(hot_ref, picked_ref):
        picked_ref[...] = lax.dot_general(
            table_ref[...], hot_ref[...], (((0,), (0,)), ((), ())), preferred_element_type=jnp.float32
        )

    def narrow(index, picked_ref):
        bundle, start, first_x, first_y = cells_of(index)
        off_y = first_y & (WIN - 1)
        off_x = first_x & (LANES - 1)
        lines = []
        for dy in range(TALL):
            parts = [picked_ref[dy * LANES + 8 * k : dy * LANES + 8 * k + 8] for k in range(LANES // 8)]
            parts.append(picked_ref[width + dy * HALO : width + (dy + 1) * HALO])
            lines.append(shift_rows(parts, off_x // 8, (8, 4, 2, 1), 2))
        low = shift_rows([line[0] for line in lines], off_y, (4, 2, 1), 4)
        high = shift_rows([line[1] for line in lines], off_y, (4, 2, 1), 4)
        patch = [shift_within(low[i], high[i], off_x)[:4].astype(jnp.int32) for i in range(4)]
        words = [(patch[i] << 16) | (patch[i + 2] & 0xFFFF) for i in range(2)]
        out_ref[bundle, :, pl.ds(start, step)] = jnp.concatenate(words, axis=0)

    total = bundles * per
    select(0, hot_a)

    def two(j, carry):
        select(2 * j + 1, hot_b)
        pick(hot_a, picked_a)
        narrow(jnp.maximum(2 * j - 1, 0), picked_b)
        select(jnp.minimum(2 * j + 2, total - 1), hot_a)
        pick(hot_b, picked_b)
        narrow(2 * j, picked_a)
        return carry

    lax.fori_loop(0, total // 2, two, 0)
    narrow(total - 1, picked_b)


def stencil_terms(patch, frac_x, frac_y):
    keep_y = 1.0 - frac_y
    level = keep_y * patch[1] + frac_y * patch[2]
    slope = (keep_y * (patch[2] - patch[0]) + frac_y * (patch[3] - patch[1])) * 0.5
    bend = keep_y * (patch[2] - 2.0 * patch[1] + patch[0]) + frac_y * (patch[3] - 2.0 * patch[2] + patch[1])
    keep_x = 1.0 - frac_x

    def across(rows):
        return [rows[k : k + 1] for k in range(4)]

    def flat(rows):
        return keep_x * rows[1] + frac_x * rows[2]

    def tilt(rows):
        return (keep_x * (rows[2] - rows[0]) + frac_x * (rows[3] - rows[1])) * 0.5

    def curve(rows):
        return keep_x * (rows[2] - 2.0 * rows[1] + rows[0]) + frac_x * (rows[3] - 2.0 * rows[2] + rows[1])

    level, slope, bend = across(level), across(slope), across(bend)
    return tilt(level), flat(slope), curve(level), flat(bend), tilt(slope)


def trace_kernel(
    plane_ref, tile_ref, slot_ref, fine_ref, root_ref, own_ref, one_ref, two_ref, three_ref, offset_ref,
    disp_ref, dist_ref, patch_ref, coarse_ref
):
    planes = tile_ref.shape[0]
    for k, ref in enumerate((own_ref, one_ref, two_ref, three_ref)):
        words = ref[...]
        half = words.shape[0]
        from_plane = (plane_ref[0] + k) & (planes - 1)
        coarse_ref[from_plane, 0:half] = (words >> 16).astype(jnp.float32)
        coarse_ref[from_plane, half : 2 * half] = ((words << 16) >> 16).astype(jnp.float32)
    slots = tile_ref.shape[1]
    rays = slot_ref.shape[1]
    step = rays

    def one(index, carry):
        plane = index // (rays // step)
        start = pl.multiple_of((index % (rays // step)) * step, step)
        slot = slot_ref[pl.ds(plane, 1), pl.ds(start, step)]
        cell = fine_ref[pl.ds(plane, 1), pl.ds(start, step)]
        ids = lax.broadcasted_iota(jnp.int32, (slots, step), 0)
        onehot = (ids == slot).astype(jnp.float32).astype(jnp.bfloat16)
        picked = lax.dot_general(
            tile_ref[plane], onehot, (((0,), (0,)), ((), ())), preferred_element_type=jnp.float32
        )
        off_x = cell % TP - 1
        off_y = cell // TP - 1
        low = shift_rows([picked[TP * y : TP * y + 8] for y in range(TP)], off_y, (8, 4, 2, 1), 4)
        high = shift_rows([picked[TP * y + 8 : TP * y + 16] for y in range(TP)], off_y, (8, 4, 2, 1), 4)
        for i in range(4):
            first = jnp.where(off_x >= 8, high[i], low[i])
            patch_ref[plane, i, :, pl.ds(start, step)] = shift_within(first, high[i], off_x)
        return carry

    lax.fori_loop(0, planes * (rays // step), one, 0, unroll=True)

    offset = [offset_ref[0:1], offset_ref[1:2]]
    disp = [jnp.zeros((1, rays), jnp.float32)] * 2
    last = disp
    zero = jnp.zeros((1, rays), jnp.float32)
    unit = jnp.ones((1, rays), jnp.float32)
    dist = [unit, zero, zero, unit]
    before = dist
    for plane in range(planes):
        chi = float(FIRST + plane)
        ahead = 2.0 * chi / (chi + 1.0)
        behind = (chi - 1.0) / (chi + 1.0)
        strength = chi / (chi + 1.0)
        position = [offset[0] + disp[0], offset[1] + disp[1]]
        fine = stencil_terms([patch_ref[plane, i] for i in range(4)], position[0], position[1])
        cell = fine_ref[plane : plane + 1]
        root = root_ref[plane : plane + 1]
        base_x = ((root % 2) * (RATIO // 2) + cell % TP).astype(jnp.float32)
        base_y = ((root // 2) * (RATIO // 2) + cell // TP).astype(jnp.float32)
        coarse = stencil_terms(
            [coarse_ref[plane, 4 * i : 4 * i + 4] for i in range(4)],
            (base_x + position[0]) * (1.0 / RATIO),
            (base_y + position[1]) * (1.0 / RATIO),
        )
        once = UNIT / RATIO
        twice = UNIT / (RATIO * RATIO)
        grad_x = fine[0] + coarse[0] * once
        grad_y = fine[1] + coarse[1] * once
        xx = fine[2] + coarse[2] * twice
        yy = fine[3] + coarse[3] * twice
        xy = fine[4] + coarse[4] * twice
        new_disp = [
            ahead * disp[0] - behind * last[0] - strength * grad_x,
            ahead * disp[1] - behind * last[1] - strength * grad_y,
        ]
        product = [
            xx * dist[0] + xy * dist[2],
            xx * dist[1] + xy * dist[3],
            xy * dist[0] + yy * dist[2],
            xy * dist[1] + yy * dist[3],
        ]
        new_dist = [ahead * dist[k] - behind * before[k] - strength * product[k] for k in range(4)]
        disp, last, dist, before = new_disp, disp, new_dist, dist
    for k in range(2):
        disp_ref[k : k + 1] = disp[k]
    for k in range(4):
        dist_ref[k : k + 1] = dist[k]


def swap(array, axes):
    return lax.all_to_all(array, axes, split_axis=0, concat_axis=0, tiled=True)


def body(
    coarse_potential,
    fine_tiles,
    tile_requests,
    ray_slot,
    fine_cell,
    coarse_cell,
    tile_root,
    ray_offset,
):
    planes = lax.axis_size("plane")
    owners = lax.axis_size("ray")
    slots = tile_requests.shape[3]
    side = coarse_potential.shape[1]
    rays = ray_offset.shape[1]
    cells = TP * TP
    vmem = pl.BlockSpec(memory_space=pltpu.VMEM)
    smem = pl.BlockSpec(memory_space=pltpu.SMEM)
    plane = jnp.full((1,), lax.axis_index("plane"), jnp.int32)

    def hop(array, by):
        return lax.ppermute(array, "plane", [(i, (i + by) % planes) for i in range(planes)])

    wishes = tile_requests[0].transpose(0, 2, 1).reshape(planes * slots, owners)
    wish_parts = [wishes] + [hop(wishes, k) for k in range(1, planes)]
    coarse_cell, *wish_parts = lax.optimization_barrier((coarse_cell, *wish_parts))
    size = coarse_potential.shape[0] * side // 2 // LANES
    message = pl.pallas_call(
        pack_kernel,
        out_shape=jax.ShapeDtypeStruct((owners, size + 8, LANES), jnp.int32),
        in_specs=[smem] + [vmem] * 5,
        out_specs=vmem,
        scratch_shapes=[pltpu.VMEM((LANES, LANES), jnp.int32)] * 2,
        name="pack",
    )(plane, coarse_potential, *wish_parts)
    messages = swap(message, "ray")
    cell_parts = [coarse_cell] + [hop(coarse_cell, k) for k in range(1, planes)]
    asked, *cell_parts = lax.optimization_barrier((messages[:, size], *cell_parts))

    outgoing = pl.pallas_call(
        take_kernel,
        out_shape=jax.ShapeDtypeStruct((planes, owners, slots, cells), jnp.bfloat16),
        in_specs=[vmem] * 2,
        out_specs=vmem,
        scratch_shapes=[pltpu.VMEM((LANES, owners), jnp.int32)],
        compiler_params=pltpu.CompilerParams(vmem_limit_bytes=32 << 20),
        cost_estimate=pl.CostEstimate(flops=1_100_000_000, bytes_accessed=1_600_000, transcendentals=0),
        name="take",
    )(asked, fine_tiles[0])
    arrived = swap(outgoing.reshape(planes * owners, slots, cells), ("plane", "ray"))

    codes = 2 * side // WIN * (side // LANES)
    step = min(512, rays)
    found = pl.pallas_call(
        coarse_kernel,
        out_shape=jax.ShapeDtypeStruct((planes, 8, rays), jnp.int32),
        in_specs=[smem] + [vmem] * 5,
        out_specs=vmem,
        scratch_shapes=[
            pltpu.VMEM((codes, (TALL + 1) * LANES), jnp.bfloat16),
            pltpu.VMEM((planes, rays), jnp.int32),
            pltpu.VMEM((codes, step), jnp.bfloat16),
            pltpu.VMEM((codes, step), jnp.bfloat16),
            pltpu.VMEM(((TALL + 1) * LANES, step), jnp.float32),
            pltpu.VMEM(((TALL + 1) * LANES, step), jnp.float32),
        ],
        compiler_params=pltpu.CompilerParams(vmem_limit_bytes=32 << 20),
        cost_estimate=pl.CostEstimate(flops=6_000_000_000, bytes_accessed=1_500_000, transcendentals=0),
        name="coarse",
    )(plane, messages, *cell_parts)
    found_parts = [found[0]] + [hop(found[k], planes - k) for k in range(1, planes)]

    return pl.pallas_call(
        trace_kernel,
        out_shape=(
            jax.ShapeDtypeStruct((2, rays), jnp.float32),
            jax.ShapeDtypeStruct((4, rays), jnp.float32),
        ),
        in_specs=[smem] + [vmem] * 9,
        out_specs=(vmem,) * 2,
        scratch_shapes=[
            pltpu.VMEM((planes, 4, 8, rays), jnp.float32),
            pltpu.VMEM((planes, 16, rays), jnp.float32),
        ],
        compiler_params=pltpu.CompilerParams(vmem_limit_bytes=32 << 20),
        cost_estimate=pl.CostEstimate(flops=1_500_000_000, bytes_accessed=1_500_000, transcendentals=0),
        name="trace",
    )(
        plane,
        arrived.reshape(planes, owners * slots, cells),
        ray_slot,
        fine_cell,
        tile_root,
        *found_parts,
        ray_offset,
    )


def solution(mesh):
    in_specs = (
        P(("plane", "ray"), None),
        P("plane", "ray", None),
        P(("plane", "ray"), None, None, None),
        P(None, ("plane", "ray")),
        P(None, ("plane", "ray")),
        P(None, ("plane", "ray")),
        P(None, ("plane", "ray")),
        P(None, ("plane", "ray")),
    )
    out_specs = (P(None, ("plane", "ray")), P(None, ("plane", "ray")))
    return jax.shard_map(body, mesh=mesh, in_specs=in_specs, out_specs=out_specs, check_vma=False)
```

```python
import jax
import jax.numpy as jnp
from jax import lax
from jax.experimental import pallas as pl
from jax.experimental.pallas import tpu as pltpu
from jax.sharding import PartitionSpec as P

TP = 16
RATIO = 32
FIRST = 31
PLANES = 4
LANES = 128
HALO = 8
WIN = 8
TALL = WIN + 3
UNIT = 72.0 / 32767.0


def shift_rows(rows, amount, bits, keep):
    left = sum(bits)
    for bit in bits:
        left -= bit
        taken = (amount & bit) != 0
        need = keep + left
        rows = [
            jnp.where(taken, rows[j + bit], rows[j]) if j + bit < len(rows) else rows[j]
            for j in range(min(need, len(rows)))
        ]
    return rows


def shift_within(low, high, amount):
    index = lax.broadcasted_iota(jnp.int32, low.shape, 0)
    far = jnp.where(index < 4, pltpu.roll(low, 4, 0), pltpu.roll(high, 4, 0))
    here = jnp.where((amount & 4) != 0, far, low)
    here = jnp.where((amount & 2) != 0, pltpu.roll(here, 6, 0), here)
    return jnp.where((amount & 1) != 0, pltpu.roll(here, 7, 0), here)


def pack_kernel(place_ref, coarse_ref, own_ref, far_ref, out_ref, wish_ref, row_ref):
    cores = 2
    slots = LANES // 8
    owners = own_ref.shape[1]
    rows = out_ref.shape[0] // (cores * owners)
    side = coarse_ref.shape[1]
    half = side // 2
    code = jnp.floor(coarse_ref[...] * (1.0 / UNIT) + 0.5).astype(jnp.int32)
    word = (code[:, :half] << 16) | (code[:, half:] & 0xFFFF)
    far = place_ref[0] // cores
    wish_ref[...] = jnp.zeros_like(wish_ref)
    for core in range(cores):
        line = pl.ds(pl.multiple_of((far * cores + core) * slots, slots), slots)
        wish_ref[pl.ds(pl.multiple_of(core * 2 * slots + far * slots, slots), slots), 0:owners] = own_ref[line, :]
        wish_ref[pl.ds(pl.multiple_of(core * 2 * slots + (1 - far) * slots, slots), slots), 0:owners] = far_ref[line, :]
    row_ref[...] = jnp.transpose(wish_ref[...])
    for core in range(cores):
        lines = row_ref[0:owners]
        lines = pltpu.roll(lines, LANES - core * 2 * slots, 1) if core else lines
        part = [word[core * WIN : (core + 1) * WIN, x * LANES : (x + 1) * LANES] for x in range(half // LANES)]
        for owner in range(owners):
            at = (core * owners + owner) * rows
            for x in range(half // LANES):
                out_ref[at + x * WIN : at + (x + 1) * WIN] = part[x]
            out_ref[at + rows - 1 : at + rows] = lines[owner : owner + 1]


def take_kernel(message_ref, tile_ref, out_ref, turned_ref):
    bundles, slots, cells = out_ref.shape
    messages = bundles // 2
    rows = message_ref.shape[0] // messages
    count = tile_ref.shape[0]
    group = 16
    asked = message_ref[pl.ds(rows - 1, messages, stride=rows), :]
    turned_ref[...] = jnp.transpose(asked)
    ids = lax.broadcasted_iota(jnp.int32, (slots, count), 1)
    for first in range(0, bundles, group):
        line = first // messages * slots
        onehot = jnp.concatenate(
            [
                (ids == turned_ref[line : line + slots, b % messages : b % messages + 1])
                .astype(jnp.float32)
                .astype(jnp.bfloat16)
                for b in range(first, first + group)
            ],
            axis=0,
        )
        got = jnp.dot(onehot, tile_ref[...], preferred_element_type=jnp.float32).astype(jnp.bfloat16)
        out_ref[first : first + group] = got.reshape(group, slots, cells)


def coarse_kernel(
    place_ref, near_ref, pair_ref, own_ref, one_ref, two_ref, three_ref, out_ref,
    table_ref, cell_ref, hot_a, hot_b, picked_a, picked_b, grid_ref
):
    plane = place_ref[0]
    core = plane & 1
    size = 2 * WIN
    owners = grid_ref.shape[0] // (2 * size)
    rows = near_ref.shape[0] // (2 * owners)
    side = owners * size
    windows = side // WIN
    chunks = side // LANES
    halves = chunks // 2
    width = TALL * LANES
    step = picked_a.shape[1]
    count = windows * chunks
    for owner in range(owners):
        first = owner * rows
        second = (owners + owner) * rows
        near = jnp.where(core == 0, near_ref[first : first + size], near_ref[second : second + size])
        pair = jnp.where(core == 0, pair_ref[first : first + size], pair_ref[second : second + size])
        grid_ref[owner * size : (owner + 1) * size] = jnp.where(core == 0, near, pair)
        grid_ref[(owners + owner) * size : (owners + owner + 1) * size] = jnp.where(core == 0, pair, near)

    def load(chunk, dy):
        parts = []
        for parity in range(2):
            pick = (parity + dy // WIN) % 2
            start = pick * owners * size + chunk % halves * WIN + dy % WIN
            part = grid_ref[pl.ds(start, owners, stride=size), :]
            if parity + dy // WIN >= 2:
                part = pltpu.roll(part, owners - 1, 0)
            parts.append(part)
        word = jnp.concatenate(parts, axis=0)
        return word >> 16 if chunk < halves else (word << 16) >> 16

    def put(code, start, column):
        high = ((code + 128) >> 8) << 8
        table_ref[pl.ds(start, windows), pl.ds(column, LANES)] = high.astype(jnp.float32).astype(jnp.bfloat16)
        table_ref[pl.ds(count + start, windows), pl.ds(column, LANES)] = (
            (code - high).astype(jnp.float32).astype(jnp.bfloat16)
        )

    lane = lax.broadcasted_iota(jnp.int32, (windows, LANES), 1)
    for chunk in range(chunks):
        base = chunk * windows
        halo = jnp.zeros((windows, LANES), jnp.int32)
        for dy in range(TALL):
            near = load((chunk + 1) % chunks, dy)
            near = pltpu.roll(near, dy * HALO, 1) if dy else near
            halo = jnp.where((lane >= dy * HALO) & (lane < (dy + 1) * HALO), near, halo)
            put(load(chunk, dy), base, dy * LANES)
        put(halo, base, width)

    for k, ref in enumerate((own_ref, one_ref, two_ref, three_ref)):
        cell_ref[k : k + 1] = ref[pl.ds(plane, 1), :]

    bundles = cell_ref.shape[0]
    per = cell_ref.shape[1] // step

    def cells_of(index):
        bundle = index // per
        start = pl.multiple_of((index % per) * step, step)
        cell = cell_ref[pl.ds(bundle, 1), pl.ds(start, step)]
        return bundle, start, (cell - 1) & (side - 1), (cell // side - 1) & (side - 1)

    def select(index, hot_ref):
        _, _, first_x, first_y = cells_of(index)
        tall = first_y // WIN
        window = (first_x // LANES) * windows + (tall & 1) * owners + tall // 2
        ids = lax.broadcasted_iota(jnp.int32, (count, step), 0)
        onehot = (ids == window).astype(jnp.float32).astype(jnp.bfloat16)
        hot_ref[0:count] = onehot
        hot_ref[count : 2 * count] = onehot

    def pick(hot_ref, picked_ref):
        picked_ref[...] = lax.dot_general(
            table_ref[...], hot_ref[...], (((0,), (0,)), ((), ())), preferred_element_type=jnp.float32
        )

    def narrow(index, picked_ref):
        bundle, start, first_x, first_y = cells_of(index)
        off_y = first_y & (WIN - 1)
        off_x = first_x & (LANES - 1)
        lines = []
        for dy in range(TALL):
            parts = [picked_ref[dy * LANES + 8 * k : dy * LANES + 8 * k + 8] for k in range(LANES // 8)]
            parts.append(picked_ref[width + dy * HALO : width + (dy + 1) * HALO])
            lines.append(shift_rows(parts, off_x // 8, (8, 4, 2, 1), 2))
        low = shift_rows([line[0] for line in lines], off_y, (4, 2, 1), 4)
        high = shift_rows([line[1] for line in lines], off_y, (4, 2, 1), 4)
        patch = [shift_within(low[i], high[i], off_x)[:4].astype(jnp.int32) for i in range(4)]
        words = [(patch[i] << 16) | (patch[i + 2] & 0xFFFF) for i in range(2)]
        out_ref[bundle, :, pl.ds(start, step)] = jnp.concatenate(words, axis=0)

    total = bundles * per
    select(0, hot_a)

    def two(j, carry):
        select(2 * j + 1, hot_b)
        pick(hot_a, picked_a)
        narrow(jnp.maximum(2 * j - 1, 0), picked_b)
        select(jnp.minimum(2 * j + 2, total - 1), hot_a)
        pick(hot_b, picked_b)
        narrow(2 * j, picked_a)
        return carry

    lax.fori_loop(0, total // 2, two, 0)
    narrow(total - 1, picked_b)


def stencil_terms(patch, frac_x, frac_y):
    keep_y = 1.0 - frac_y
    level = keep_y * patch[1] + frac_y * patch[2]
    slope = (keep_y * (patch[2] - patch[0]) + frac_y * (patch[3] - patch[1])) * 0.5
    bend = keep_y * (patch[2] - 2.0 * patch[1] + patch[0]) + frac_y * (patch[3] - 2.0 * patch[2] + patch[1])
    keep_x = 1.0 - frac_x

    def across(rows):
        return [rows[k : k + 1] for k in range(4)]

    def flat(rows):
        return keep_x * rows[1] + frac_x * rows[2]

    def tilt(rows):
        return (keep_x * (rows[2] - rows[0]) + frac_x * (rows[3] - rows[1])) * 0.5

    def curve(rows):
        return keep_x * (rows[2] - 2.0 * rows[1] + rows[0]) + frac_x * (rows[3] - 2.0 * rows[2] + rows[1])

    level, slope, bend = across(level), across(slope), across(bend)
    return tilt(level), flat(slope), curve(level), flat(bend), tilt(slope)


def trace_kernel(
    plane_ref, tile_ref, slot_ref, fine_ref, root_ref, own_ref, one_ref, two_ref, three_ref, offset_ref,
    disp_ref, dist_ref, patch_ref, coarse_ref
):
    planes = tile_ref.shape[0]
    for k, ref in enumerate((own_ref, one_ref, two_ref, three_ref)):
        words = ref[...]
        half = words.shape[0]
        from_plane = (plane_ref[0] + k) & (planes - 1)
        coarse_ref[from_plane, 0:half] = (words >> 16).astype(jnp.float32)
        coarse_ref[from_plane, half : 2 * half] = ((words << 16) >> 16).astype(jnp.float32)
    slots = tile_ref.shape[1]
    rays = slot_ref.shape[1]
    step = rays

    def one(index, carry):
        plane = index // (rays // step)
        start = pl.multiple_of((index % (rays // step)) * step, step)
        slot = slot_ref[pl.ds(plane, 1), pl.ds(start, step)]
        cell = fine_ref[pl.ds(plane, 1), pl.ds(start, step)]
        ids = lax.broadcasted_iota(jnp.int32, (slots, step), 0)
        onehot = (ids == slot).astype(jnp.float32).astype(jnp.bfloat16)
        picked = lax.dot_general(
            tile_ref[plane], onehot, (((0,), (0,)), ((), ())), preferred_element_type=jnp.float32
        )
        off_x = cell % TP - 1
        off_y = cell // TP - 1
        low = shift_rows([picked[TP * y : TP * y + 8] for y in range(TP)], off_y, (8, 4, 2, 1), 4)
        high = shift_rows([picked[TP * y + 8 : TP * y + 16] for y in range(TP)], off_y, (8, 4, 2, 1), 4)
        for i in range(4):
            first = jnp.where(off_x >= 8, high[i], low[i])
            patch_ref[plane, i, :, pl.ds(start, step)] = shift_within(first, high[i], off_x)
        return carry

    lax.fori_loop(0, planes * (rays // step), one, 0, unroll=True)

    offset = [offset_ref[0:1], offset_ref[1:2]]
    disp = [jnp.zeros((1, rays), jnp.float32)] * 2
    last = disp
    zero = jnp.zeros((1, rays), jnp.float32)
    unit = jnp.ones((1, rays), jnp.float32)
    dist = [unit, zero, zero, unit]
    before = dist
    for plane in range(planes):
        chi = float(FIRST + plane)
        ahead = 2.0 * chi / (chi + 1.0)
        behind = (chi - 1.0) / (chi + 1.0)
        strength = chi / (chi + 1.0)
        position = [offset[0] + disp[0], offset[1] + disp[1]]
        fine = stencil_terms([patch_ref[plane, i] for i in range(4)], position[0], position[1])
        cell = fine_ref[plane : plane + 1]
        root = root_ref[plane : plane + 1]
        base_x = ((root % 2) * (RATIO // 2) + cell % TP).astype(jnp.float32)
        base_y = ((root // 2) * (RATIO // 2) + cell // TP).astype(jnp.float32)
        coarse = stencil_terms(
            [coarse_ref[plane, 4 * i : 4 * i + 4] for i in range(4)],
            (base_x + position[0]) * (1.0 / RATIO),
            (base_y + position[1]) * (1.0 / RATIO),
        )
        once = UNIT / RATIO
        twice = UNIT / (RATIO * RATIO)
        grad_x = fine[0] + coarse[0] * once
        grad_y = fine[1] + coarse[1] * once
        xx = fine[2] + coarse[2] * twice
        yy = fine[3] + coarse[3] * twice
        xy = fine[4] + coarse[4] * twice
        new_disp = [
            ahead * disp[0] - behind * last[0] - strength * grad_x,
            ahead * disp[1] - behind * last[1] - strength * grad_y,
        ]
        product = [
            xx * dist[0] + xy * dist[2],
            xx * dist[1] + xy * dist[3],
            xy * dist[0] + yy * dist[2],
            xy * dist[1] + yy * dist[3],
        ]
        new_dist = [ahead * dist[k] - behind * before[k] - strength * product[k] for k in range(4)]
        disp, last, dist, before = new_disp, disp, new_dist, dist
    for k in range(2):
        disp_ref[k : k + 1] = disp[k]
    for k in range(4):
        dist_ref[k : k + 1] = dist[k]


def swap(array, axes):
    return lax.all_to_all(array, axes, split_axis=0, concat_axis=0, tiled=True)


def body(
    coarse_potential,
    fine_tiles,
    tile_requests,
    ray_slot,
    fine_cell,
    coarse_cell,
    tile_root,
    ray_offset,
):
    planes = lax.axis_size("plane")
    owners = lax.axis_size("ray")
    slots = tile_requests.shape[3]
    side = coarse_potential.shape[1]
    rays = ray_offset.shape[1]
    cells = TP * TP
    vmem = pl.BlockSpec(memory_space=pltpu.VMEM)
    smem = pl.BlockSpec(memory_space=pltpu.SMEM)
    place = jnp.full((1,), lax.axis_index("plane"), jnp.int32)

    def hop(array, by):
        return lax.ppermute(array, "plane", [(i, (i + by) % planes) for i in range(planes)])

    wishes = tile_requests[0].transpose(0, 2, 1).reshape(planes * slots, owners)
    coarse_cell, far_wishes = lax.optimization_barrier((coarse_cell, hop(wishes, 2)))
    rows = coarse_potential.shape[0] // 2 * (side // 2) // LANES + 1
    wide = planes // 2 * owners
    message = pl.pallas_call(
        pack_kernel,
        out_shape=jax.ShapeDtypeStruct((wide * rows, LANES), jnp.int32),
        in_specs=[smem] + [vmem] * 3,
        out_specs=vmem,
        scratch_shapes=[pltpu.VMEM((LANES, LANES), jnp.int32)] * 2,
        name="pack",
    )(place, coarse_potential, wishes, far_wishes)
    messages = lax.all_to_all(
        message.reshape(wide * rows, 1, LANES),
        ("plane", "ray"),
        split_axis=0,
        concat_axis=0,
        tiled=True,
        axis_index_groups=[list(range(k * wide, (k + 1) * wide)) for k in range(2)],
    ).reshape(wide * rows, LANES)
    cell_parts = [coarse_cell] + [hop(coarse_cell, k) for k in range(1, planes)]
    messages, *cell_parts = lax.optimization_barrier((messages, *cell_parts))
    pair_messages = lax.ppermute(messages, "plane", [(i, i ^ 1) for i in range(planes)])
    outgoing = pl.pallas_call(
        take_kernel,
        out_shape=jax.ShapeDtypeStruct((planes * owners, slots, cells), jnp.bfloat16),
        in_specs=[vmem] * 2,
        out_specs=vmem,
        scratch_shapes=[pltpu.VMEM((LANES, wide), jnp.int32)],
        compiler_params=pltpu.CompilerParams(vmem_limit_bytes=32 << 20),
        cost_estimate=pl.CostEstimate(flops=1_100_000_000, bytes_accessed=1_600_000, transcendentals=0),
        name="take",
    )(messages, fine_tiles[0])
    arrived = swap(outgoing, ("plane", "ray"))

    codes = 2 * side // WIN * (side // LANES)
    step = min(512, rays)
    found = pl.pallas_call(
        coarse_kernel,
        out_shape=jax.ShapeDtypeStruct((planes, 8, rays), jnp.int32),
        in_specs=[smem] + [vmem] * 6,
        out_specs=vmem,
        scratch_shapes=[
            pltpu.VMEM((codes, (TALL + 1) * LANES), jnp.bfloat16),
            pltpu.VMEM((planes, rays), jnp.int32),
            pltpu.VMEM((codes, step), jnp.bfloat16),
            pltpu.VMEM((codes, step), jnp.bfloat16),
            pltpu.VMEM(((TALL + 1) * LANES, step), jnp.float32),
            pltpu.VMEM(((TALL + 1) * LANES, step), jnp.float32),
            pltpu.VMEM((wide * (rows - 1), LANES), jnp.int32),
        ],
        compiler_params=pltpu.CompilerParams(vmem_limit_bytes=32 << 20),
        cost_estimate=pl.CostEstimate(flops=6_000_000_000, bytes_accessed=1_500_000, transcendentals=0),
        name="coarse",
    )(place, messages, pair_messages, *cell_parts)
    found_parts = [found[0]] + [hop(found[k], planes - k) for k in range(1, planes)]

    return pl.pallas_call(
        trace_kernel,
        out_shape=(
            jax.ShapeDtypeStruct((2, rays), jnp.float32),
            jax.ShapeDtypeStruct((4, rays), jnp.float32),
        ),
        in_specs=[smem] + [vmem] * 9,
        out_specs=(vmem,) * 2,
        scratch_shapes=[
            pltpu.VMEM((planes, 4, 8, rays), jnp.float32),
            pltpu.VMEM((planes, 16, rays), jnp.float32),
        ],
        compiler_params=pltpu.CompilerParams(vmem_limit_bytes=32 << 20),
        cost_estimate=pl.CostEstimate(flops=1_500_000_000, bytes_accessed=1_500_000, transcendentals=0),
        name="trace",
    )(
        place,
        arrived.reshape(planes, owners * slots, cells),
        ray_slot,
        fine_cell,
        tile_root,
        *found_parts,
        ray_offset,
    )


def solution(mesh):
    in_specs = (
        P(("plane", "ray"), None),
        P("plane", "ray", None),
        P(("plane", "ray"), None, None, None),
        P(None, ("plane", "ray")),
        P(None, ("plane", "ray")),
        P(None, ("plane", "ray")),
        P(None, ("plane", "ray")),
        P(None, ("plane", "ray")),
    )
    out_specs = (P(None, ("plane", "ray")), P(None, ("plane", "ray")))
    return jax.shard_map(body, mesh=mesh, in_specs=in_specs, out_specs=out_specs, check_vma=False)
```

```python
import math

import jax
import jax.numpy as jnp
from jax import lax
from jax.experimental import pallas as pl
from jax.experimental.pallas import tpu as pltpu
from jax.sharding import PartitionSpec as P

TP = 16
RATIO = 32
FIRST = 31
PLANES = 4
LANES = 128
HALO = 8
WIN = 8
TALL = WIN + 3
UNIT = 72.0 / 32767.0


def shift_rows(rows, amount, bits, keep):
    left = sum(bits)
    for bit in bits:
        left -= bit
        taken = (amount & bit) != 0
        need = keep + left
        rows = [
            jnp.where(taken, rows[j + bit], rows[j]) if j + bit < len(rows) else rows[j]
            for j in range(min(need, len(rows)))
        ]
    return rows


def shift_within(low, high, amount):
    index = lax.broadcasted_iota(jnp.int32, low.shape, 0)
    far = jnp.where(index < 4, pltpu.roll(low, 4, 0), pltpu.roll(high, 4, 0))
    here = jnp.where((amount & 4) != 0, far, low)
    here = jnp.where((amount & 2) != 0, pltpu.roll(here, 6, 0), here)
    return jnp.where((amount & 1) != 0, pltpu.roll(here, 7, 0), here)


def pack_kernel(plane_ref, coarse_ref, own_ref, one_ref, two_ref, three_ref, out_ref, wish_ref, row_ref):
    owners = own_ref.shape[1]
    rows = out_ref.shape[0] // owners
    planes = PLANES
    slots = own_ref.shape[0] // planes
    side = coarse_ref.shape[1]
    half = side // 2
    code = jnp.floor(coarse_ref[...] * (1.0 / UNIT) + 0.5).astype(jnp.int32)
    word = (code[:, :half] << 16) | (code[:, half:] & 0xFFFF)
    tiles = []
    for y in range(coarse_ref.shape[0] // WIN):
        for x in range(half // LANES):
            tiles.append(word[y * WIN : (y + 1) * WIN, x * LANES : (x + 1) * LANES])
    block = jnp.concatenate(tiles, axis=0)
    plane = plane_ref[0]
    wish_ref[...] = jnp.zeros_like(wish_ref)
    for k, ref in enumerate((own_ref, one_ref, two_ref, three_ref)):
        source = (plane + planes - k) & (planes - 1)
        wish_ref[pl.ds(pl.multiple_of(source * slots, slots), slots), 0:owners] = ref[
            pl.ds(pl.multiple_of(plane * slots, slots), slots), :
        ]
    row_ref[...] = jnp.transpose(wish_ref[...])
    for owner in range(owners):
        at = owner * rows
        out_ref[at : at + rows - 1] = block
        out_ref[at + rows - 1 : at + rows] = row_ref[owner : owner + 1]


def take_kernel(asked_ref, tile_ref, out_ref, turned_ref, held_ref, sems):
    planes, owners, slots, cells = out_ref.shape
    count = tile_ref.shape[0]
    lot = planes * slots
    group = 4
    copies = []
    rows = asked_ref.shape[0] // owners
    turned_ref[...] = jnp.transpose(asked_ref[pl.ds(rows - 1, owners, stride=rows), :])
    ids = lax.broadcasted_iota(jnp.int32, (lot, count), 1)
    for first in range(0, owners, group):
        onehot = jnp.concatenate(
            [
                (ids == turned_ref[0:lot, r : r + 1]).astype(jnp.float32).astype(jnp.bfloat16)
                for r in range(first, first + group)
            ],
            axis=0,
        )
        got = jnp.dot(onehot, tile_ref[...], preferred_element_type=jnp.float32).astype(jnp.bfloat16)
        for r in range(group):
            for p in range(planes):
                start = r * lot + p * slots
                held_ref[p, first + r] = got[start : start + slots]
        for p in range(planes):
            copies.append(
                pltpu.make_async_copy(
                    held_ref.at[p, first : first + group], out_ref.at[p, first : first + group], sems.at[p, first // group]
                )
            )
            copies[-1].start()
    for copy in copies:
        copy.wait()


def coarse_kernel(
    plane_ref, grid_ref, own_ref, one_ref, two_ref, three_ref, out_ref,
    table_ref, cell_ref, hot_a, hot_b, picked_a, picked_b
):
    plane = plane_ref[0]
    side = math.isqrt(table_ref.shape[0] // 2 * WIN * LANES)
    owners = side // (2 * WIN)
    rows = grid_ref.shape[0] // owners
    windows = side // WIN
    chunks = side // LANES
    halves = chunks // 2
    width = TALL * LANES
    step = picked_a.shape[1]
    count = windows * chunks
    grid = grid_ref

    def load(chunk, dy):
        parts = []
        for parity in range(2):
            pick = (parity + dy // WIN) % 2
            start = (pick * halves + chunk % halves) * WIN + dy % WIN
            part = grid[pl.ds(start, owners, stride=rows), :]
            if parity + dy // WIN >= 2:
                part = pltpu.roll(part, owners - 1, 0)
            parts.append(part)
        word = jnp.concatenate(parts, axis=0)
        return word >> 16 if chunk < halves else (word << 16) >> 16

    def put(code, start, column):
        high = ((code + 128) >> 8) << 8
        table_ref[pl.ds(start, windows), pl.ds(column, LANES)] = high.astype(jnp.float32).astype(jnp.bfloat16)
        table_ref[pl.ds(count + start, windows), pl.ds(column, LANES)] = (
            (code - high).astype(jnp.float32).astype(jnp.bfloat16)
        )

    lane = lax.broadcasted_iota(jnp.int32, (windows, LANES), 1)
    for chunk in range(chunks):
        base = chunk * windows
        halo = jnp.zeros((windows, LANES), jnp.int32)
        for dy in range(TALL):
            near = load((chunk + 1) % chunks, dy)
            near = pltpu.roll(near, dy * HALO, 1) if dy else near
            halo = jnp.where((lane >= dy * HALO) & (lane < (dy + 1) * HALO), near, halo)
            put(load(chunk, dy), base, dy * LANES)
        put(halo, base, width)

    for k, ref in enumerate((own_ref, one_ref, two_ref, three_ref)):
        cell_ref[k : k + 1] = ref[...]

    bundles = cell_ref.shape[0]
    per = cell_ref.shape[1] // step

    def cells_of(index):
        bundle = index // per
        start = pl.multiple_of((index % per) * step, step)
        cell = cell_ref[pl.ds(bundle, 1), pl.ds(start, step)]
        return bundle, start, (cell - 1) & (side - 1), (cell // side - 1) & (side - 1)

    def select(index, hot_ref):
        _, _, first_x, first_y = cells_of(index)
        tall = first_y // WIN
        window = (first_x // LANES) * windows + (tall & 1) * owners + tall // 2
        ids = lax.broadcasted_iota(jnp.int32, (count, step), 0)
        onehot = (ids == window).astype(jnp.float32).astype(jnp.bfloat16)
        hot_ref[0:count] = onehot
        hot_ref[count : 2 * count] = onehot

    def pick(hot_ref, picked_ref):
        picked_ref[...] = lax.dot_general(
            table_ref[...], hot_ref[...], (((0,), (0,)), ((), ())), preferred_element_type=jnp.float32
        )

    def narrow(index, picked_ref):
        bundle, start, first_x, first_y = cells_of(index)
        off_y = first_y & (WIN - 1)
        off_x = first_x & (LANES - 1)
        lines = []
        for dy in range(TALL):
            parts = [picked_ref[dy * LANES + 8 * k : dy * LANES + 8 * k + 8] for k in range(LANES // 8)]
            parts.append(picked_ref[width + dy * HALO : width + (dy + 1) * HALO])
            lines.append(shift_rows(parts, off_x // 8, (8, 4, 2, 1), 2))
        low = shift_rows([line[0] for line in lines], off_y, (4, 2, 1), 4)
        high = shift_rows([line[1] for line in lines], off_y, (4, 2, 1), 4)
        patch = [shift_within(low[i], high[i], off_x)[:4].astype(jnp.int32) for i in range(4)]
        words = [(patch[i] << 16) | (patch[i + 2] & 0xFFFF) for i in range(2)]
        out_ref[bundle, :, pl.ds(start, step)] = jnp.concatenate(words, axis=0)

    total = bundles * per
    select(0, hot_a)

    def two(j, carry):
        select(2 * j + 1, hot_b)
        pick(hot_a, picked_a)
        narrow(jnp.maximum(2 * j - 1, 0), picked_b)
        select(jnp.minimum(2 * j + 2, total - 1), hot_a)
        pick(hot_b, picked_b)
        narrow(2 * j, picked_a)
        return carry

    lax.fori_loop(0, total // 2, two, 0)
    narrow(total - 1, picked_b)


def stencil_terms(patch, frac_x, frac_y):
    keep_y = 1.0 - frac_y
    level = keep_y * patch[1] + frac_y * patch[2]
    slope = (keep_y * (patch[2] - patch[0]) + frac_y * (patch[3] - patch[1])) * 0.5
    bend = keep_y * (patch[2] - 2.0 * patch[1] + patch[0]) + frac_y * (patch[3] - 2.0 * patch[2] + patch[1])
    keep_x = 1.0 - frac_x

    def across(rows):
        return [rows[k : k + 1] for k in range(4)]

    def flat(rows):
        return keep_x * rows[1] + frac_x * rows[2]

    def tilt(rows):
        return (keep_x * (rows[2] - rows[0]) + frac_x * (rows[3] - rows[1])) * 0.5

    def curve(rows):
        return keep_x * (rows[2] - 2.0 * rows[1] + rows[0]) + frac_x * (rows[3] - 2.0 * rows[2] + rows[1])

    level, slope, bend = across(level), across(slope), across(bend)
    return tilt(level), flat(slope), curve(level), flat(bend), tilt(slope)


def trace_kernel(
    plane_ref, tile_ref, slot_ref, fine_ref, root_ref, own_ref, one_ref, two_ref, three_ref, offset_ref,
    disp_ref, dist_ref, patch_ref, coarse_ref
):
    planes = tile_ref.shape[0]
    for k, ref in enumerate((own_ref, one_ref, two_ref, three_ref)):
        words = ref[...]
        half = words.shape[0]
        from_plane = (plane_ref[0] + k) & (planes - 1)
        coarse_ref[from_plane, 0:half] = (words >> 16).astype(jnp.float32)
        coarse_ref[from_plane, half : 2 * half] = ((words << 16) >> 16).astype(jnp.float32)
    slots = tile_ref.shape[1]
    rays = slot_ref.shape[1]
    step = rays

    def one(index, carry):
        plane = index // (rays // step)
        start = pl.multiple_of((index % (rays // step)) * step, step)
        slot = slot_ref[pl.ds(plane, 1), pl.ds(start, step)]
        cell = fine_ref[pl.ds(plane, 1), pl.ds(start, step)]
        ids = lax.broadcasted_iota(jnp.int32, (slots, step), 0)
        onehot = (ids == slot).astype(jnp.float32).astype(jnp.bfloat16)
        picked = lax.dot_general(
            tile_ref[plane], onehot, (((0,), (0,)), ((), ())), preferred_element_type=jnp.float32
        )
        off_x = cell % TP - 1
        off_y = cell // TP - 1
        low = shift_rows([picked[TP * y : TP * y + 8] for y in range(TP)], off_y, (8, 4, 2, 1), 4)
        high = shift_rows([picked[TP * y + 8 : TP * y + 16] for y in range(TP)], off_y, (8, 4, 2, 1), 4)
        for i in range(4):
            first = jnp.where(off_x >= 8, high[i], low[i])
            patch_ref[plane, i, :, pl.ds(start, step)] = shift_within(first, high[i], off_x)
        return carry

    lax.fori_loop(0, planes * (rays // step), one, 0, unroll=True)

    offset = [offset_ref[0:1], offset_ref[1:2]]
    disp = [jnp.zeros((1, rays), jnp.float32)] * 2
    last = disp
    zero = jnp.zeros((1, rays), jnp.float32)
    unit = jnp.ones((1, rays), jnp.float32)
    dist = [unit, zero, zero, unit]
    before = dist
    for plane in range(planes):
        chi = float(FIRST + plane)
        ahead = 2.0 * chi / (chi + 1.0)
        behind = (chi - 1.0) / (chi + 1.0)
        strength = chi / (chi + 1.0)
        position = [offset[0] + disp[0], offset[1] + disp[1]]
        fine = stencil_terms([patch_ref[plane, i] for i in range(4)], position[0], position[1])
        cell = fine_ref[plane : plane + 1]
        root = root_ref[plane : plane + 1]
        base_x = ((root % 2) * (RATIO // 2) + cell % TP).astype(jnp.float32)
        base_y = ((root // 2) * (RATIO // 2) + cell // TP).astype(jnp.float32)
        coarse = stencil_terms(
            [coarse_ref[plane, 4 * i : 4 * i + 4] for i in range(4)],
            (base_x + position[0]) * (1.0 / RATIO),
            (base_y + position[1]) * (1.0 / RATIO),
        )
        once = UNIT / RATIO
        twice = UNIT / (RATIO * RATIO)
        grad_x = fine[0] + coarse[0] * once
        grad_y = fine[1] + coarse[1] * once
        xx = fine[2] + coarse[2] * twice
        yy = fine[3] + coarse[3] * twice
        xy = fine[4] + coarse[4] * twice
        new_disp = [
            ahead * disp[0] - behind * last[0] - strength * grad_x,
            ahead * disp[1] - behind * last[1] - strength * grad_y,
        ]
        product = [
            xx * dist[0] + xy * dist[2],
            xx * dist[1] + xy * dist[3],
            xy * dist[0] + yy * dist[2],
            xy * dist[1] + yy * dist[3],
        ]
        new_dist = [ahead * dist[k] - behind * before[k] - strength * product[k] for k in range(4)]
        disp, last, dist, before = new_disp, disp, new_dist, dist
    for k in range(2):
        disp_ref[k : k + 1] = disp[k]
    for k in range(4):
        dist_ref[k : k + 1] = dist[k]


def swap(array, axes):
    return lax.all_to_all(array, axes, split_axis=0, concat_axis=0, tiled=True)


def body(
    coarse_potential,
    fine_tiles,
    tile_requests,
    ray_slot,
    fine_cell,
    coarse_cell,
    tile_root,
    ray_offset,
):
    planes = lax.axis_size("plane")
    owners = lax.axis_size("ray")
    slots = tile_requests.shape[3]
    side = coarse_potential.shape[1]
    rays = ray_offset.shape[1]
    cells = TP * TP
    vmem = pl.BlockSpec(memory_space=pltpu.VMEM)
    smem = pl.BlockSpec(memory_space=pltpu.SMEM)
    plane = jnp.full((1,), lax.axis_index("plane"), jnp.int32)

    def hop(array, by):
        return lax.ppermute(array, "plane", [(i, (i + by) % planes) for i in range(planes)])

    wishes = tile_requests[0].transpose(0, 2, 1).reshape(planes * slots, owners)
    wish_parts = [wishes] + [hop(wishes, k) for k in range(1, planes)]
    coarse_cell, *wish_parts = lax.optimization_barrier((coarse_cell, *wish_parts))
    size = coarse_potential.shape[0] * side // 2 // LANES
    message = pl.pallas_call(
        pack_kernel,
        out_shape=jax.ShapeDtypeStruct((owners * (size + 1), LANES), jnp.int32),
        in_specs=[smem] + [vmem] * 5,
        out_specs=vmem,
        scratch_shapes=[pltpu.VMEM((LANES, LANES), jnp.int32)] * 2,
        name="pack",
    )(plane, coarse_potential, *wish_parts)
    messages = swap(message.reshape(-1, 1, LANES), "ray").reshape(-1, LANES)
    at = lax.axis_index("plane")
    cell_rows = [lax.dynamic_slice(coarse_cell, ((at + k) % planes, 0), (1, rays)) for k in range(planes)]
    cell_parts = [cell_rows[0]] + [hop(cell_rows[k], k) for k in range(1, planes)]
    messages, *cell_parts = lax.optimization_barrier((messages, *cell_parts))

    outgoing = pl.pallas_call(
        take_kernel,
        out_shape=jax.ShapeDtypeStruct((planes, owners, slots, cells), jnp.bfloat16),
        in_specs=[vmem] * 2,
        out_specs=pl.BlockSpec(memory_space=pl.ANY),
        scratch_shapes=[
            pltpu.VMEM((LANES, owners), jnp.int32),
            pltpu.VMEM((planes, owners, slots, cells), jnp.bfloat16),
            pltpu.SemaphoreType.DMA((planes, owners // 4)),
        ],
        compiler_params=pltpu.CompilerParams(vmem_limit_bytes=32 << 20),
        cost_estimate=pl.CostEstimate(flops=1_100_000_000, bytes_accessed=1_600_000, transcendentals=0),
        name="take",
    )(messages, fine_tiles[0])
    arrived = swap(outgoing.reshape(planes * owners, slots, cells), ("plane", "ray"))

    codes = 2 * side // WIN * (side // LANES)
    step = min(512, rays)
    found = pl.pallas_call(
        coarse_kernel,
        out_shape=jax.ShapeDtypeStruct((planes, 8, rays), jnp.int32),
        in_specs=[smem] + [vmem] * 5,
        out_specs=vmem,
        scratch_shapes=[
            pltpu.VMEM((codes, (TALL + 1) * LANES), jnp.bfloat16),
            pltpu.VMEM((planes, rays), jnp.int32),
            pltpu.VMEM((codes, step), jnp.bfloat16),
            pltpu.VMEM((codes, step), jnp.bfloat16),
            pltpu.VMEM(((TALL + 1) * LANES, step), jnp.float32),
            pltpu.VMEM(((TALL + 1) * LANES, step), jnp.float32),
        ],
        compiler_params=pltpu.CompilerParams(vmem_limit_bytes=32 << 20),
        cost_estimate=pl.CostEstimate(flops=6_000_000_000, bytes_accessed=1_500_000, transcendentals=0),
        name="coarse",
    )(plane, messages, *cell_parts)
    found_parts = [found[0]] + [hop(found[k], planes - k) for k in range(1, planes)]

    return pl.pallas_call(
        trace_kernel,
        out_shape=(
            jax.ShapeDtypeStruct((2, rays), jnp.float32),
            jax.ShapeDtypeStruct((4, rays), jnp.float32),
        ),
        in_specs=[smem] + [vmem] * 9,
        out_specs=(vmem,) * 2,
        scratch_shapes=[
            pltpu.VMEM((planes, 4, 8, rays), jnp.float32),
            pltpu.VMEM((planes, 16, rays), jnp.float32),
        ],
        compiler_params=pltpu.CompilerParams(vmem_limit_bytes=32 << 20),
        cost_estimate=pl.CostEstimate(flops=1_500_000_000, bytes_accessed=1_500_000, transcendentals=0),
        name="trace",
    )(
        plane,
        arrived.reshape(planes, owners * slots, cells),
        ray_slot,
        fine_cell,
        tile_root,
        *found_parts,
        ray_offset,
    )


def solution(mesh):
    in_specs = (
        P(("plane", "ray"), None),
        P("plane", "ray", None),
        P(("plane", "ray"), None, None, None),
        P(None, ("plane", "ray")),
        P(None, ("plane", "ray")),
        P(None, ("plane", "ray")),
        P(None, ("plane", "ray")),
        P(None, ("plane", "ray")),
    )
    out_specs = (P(None, ("plane", "ray")), P(None, ("plane", "ray")))
    return jax.shard_map(body, mesh=mesh, in_specs=in_specs, out_specs=out_specs, check_vma=False)
```

```python
import math

import jax
import jax.numpy as jnp
from jax import lax
from jax.experimental import pallas as pl
from jax.experimental.pallas import tpu as pltpu
from jax.sharding import PartitionSpec as P

TP = 16
RATIO = 32
FIRST = 31
PLANES = 4
LANES = 128
HALO = 8
WIN = 8
TALL = WIN + 3
UNIT = 72.0 / 32767.0


def shift_rows(rows, amount, bits, keep):
    left = sum(bits)
    for bit in bits:
        left -= bit
        taken = (amount & bit) != 0
        need = keep + left
        rows = [
            jnp.where(taken, rows[j + bit], rows[j]) if j + bit < len(rows) else rows[j]
            for j in range(min(need, len(rows)))
        ]
    return rows


def shift_within(low, high, amount):
    index = lax.broadcasted_iota(jnp.int32, low.shape, 0)
    far = jnp.where(index < 4, pltpu.roll(low, 4, 0), pltpu.roll(high, 4, 0))
    here = jnp.where((amount & 4) != 0, far, low)
    here = jnp.where((amount & 2) != 0, pltpu.roll(here, 6, 0), here)
    return jnp.where((amount & 1) != 0, pltpu.roll(here, 7, 0), here)


def pack_kernel(coarse_ref, own_ref, one_ref, two_ref, three_ref, out_ref, wish_ref, row_ref):
    owners = own_ref.shape[1]
    rows = out_ref.shape[0] // owners
    planes = PLANES
    slots = own_ref.shape[0] // planes
    side = coarse_ref.shape[1]
    half = side // 2
    code = jnp.floor(coarse_ref[...] * (1.0 / UNIT) + 0.5).astype(jnp.int32)
    word = (code[:, :half] << 16) | (code[:, half:] & 0xFFFF)
    tiles = []
    for y in range(coarse_ref.shape[0] // WIN):
        for x in range(half // LANES):
            tiles.append(word[y * WIN : (y + 1) * WIN, x * LANES : (x + 1) * LANES])
    block = jnp.concatenate(tiles, axis=0)
    plane = lax.axis_index("plane")
    wish_ref[...] = jnp.zeros_like(wish_ref)
    for k, ref in enumerate((own_ref, one_ref, two_ref, three_ref)):
        source = (plane + planes - k) & (planes - 1)
        wish_ref[pl.ds(pl.multiple_of(source * slots, slots), slots), 0:owners] = ref[
            pl.ds(pl.multiple_of(plane * slots, slots), slots), :
        ]
    row_ref[...] = jnp.transpose(wish_ref[...])
    for owner in range(owners):
        at = owner * rows
        out_ref[at : at + rows - 1] = block
        out_ref[at + rows - 1 : at + rows] = row_ref[owner : owner + 1]


def take_kernel(asked_ref, tile_ref, out_ref, turned_ref, held_ref, sems):
    planes, owners, slots, cells = out_ref.shape
    count = tile_ref.shape[0]
    lot = planes * slots
    group = 4
    copies = []
    rows = asked_ref.shape[0] // owners
    turned_ref[...] = jnp.transpose(asked_ref[pl.ds(rows - 1, owners, stride=rows), :])
    ids = lax.broadcasted_iota(jnp.int32, (lot, count), 1)
    for first in range(0, owners, group):
        onehot = jnp.concatenate(
            [
                (ids == turned_ref[0:lot, r : r + 1]).astype(jnp.float32).astype(jnp.bfloat16)
                for r in range(first, first + group)
            ],
            axis=0,
        )
        got = jnp.dot(onehot, tile_ref[...], preferred_element_type=jnp.float32).astype(jnp.bfloat16)
        for r in range(group):
            for p in range(planes):
                start = r * lot + p * slots
                held_ref[p, first + r] = got[start : start + slots]
        for p in range(planes):
            copies.append(
                pltpu.make_async_copy(
                    held_ref.at[p, first : first + group], out_ref.at[p, first : first + group], sems.at[p, first // group]
                )
            )
            copies[-1].start()
    for copy in copies:
        copy.wait()


def coarse_kernel(
    grid_ref, own_ref, one_ref, two_ref, three_ref, out_ref,
    table_ref, cell_ref, hot_a, hot_b, picked_a, picked_b
):
    plane = lax.axis_index("plane")
    side = math.isqrt(table_ref.shape[0] // 2 * WIN * LANES)
    owners = side // (2 * WIN)
    rows = grid_ref.shape[0] // owners
    windows = side // WIN
    chunks = side // LANES
    halves = chunks // 2
    width = TALL * LANES
    step = picked_a.shape[1]
    count = windows * chunks
    grid = grid_ref

    def load(chunk, dy):
        parts = []
        for parity in range(2):
            pick = (parity + dy // WIN) % 2
            start = (pick * halves + chunk % halves) * WIN + dy % WIN
            part = grid[pl.ds(start, owners, stride=rows), :]
            if parity + dy // WIN >= 2:
                part = pltpu.roll(part, owners - 1, 0)
            parts.append(part)
        word = jnp.concatenate(parts, axis=0)
        return word >> 16 if chunk < halves else (word << 16) >> 16

    def put(code, start, column):
        high = ((code + 128) >> 8) << 8
        table_ref[pl.ds(start, windows), pl.ds(column, LANES)] = high.astype(jnp.float32).astype(jnp.bfloat16)
        table_ref[pl.ds(count + start, windows), pl.ds(column, LANES)] = (
            (code - high).astype(jnp.float32).astype(jnp.bfloat16)
        )

    lane = lax.broadcasted_iota(jnp.int32, (windows, LANES), 1)
    for chunk in range(chunks):
        base = chunk * windows
        halo = jnp.zeros((windows, LANES), jnp.int32)
        for dy in range(TALL):
            near = load((chunk + 1) % chunks, dy)
            near = pltpu.roll(near, dy * HALO, 1) if dy else near
            halo = jnp.where((lane >= dy * HALO) & (lane < (dy + 1) * HALO), near, halo)
            put(load(chunk, dy), base, dy * LANES)
        put(halo, base, width)

    for k, ref in enumerate((own_ref, one_ref, two_ref, three_ref)):
        cell_ref[k : k + 1] = ref[...]

    bundles = cell_ref.shape[0]
    per = cell_ref.shape[1] // step

    def cells_of(index):
        bundle = index // per
        start = pl.multiple_of((index % per) * step, step)
        cell = cell_ref[pl.ds(bundle, 1), pl.ds(start, step)]
        return bundle, start, (cell - 1) & (side - 1), (cell // side - 1) & (side - 1)

    def select(index, hot_ref):
        _, _, first_x, first_y = cells_of(index)
        tall = first_y // WIN
        window = (first_x // LANES) * windows + (tall & 1) * owners + tall // 2
        ids = lax.broadcasted_iota(jnp.int32, (count, step), 0)
        onehot = (ids == window).astype(jnp.float32).astype(jnp.bfloat16)
        hot_ref[0:count] = onehot
        hot_ref[count : 2 * count] = onehot

    def pick(hot_ref, picked_ref):
        picked_ref[...] = lax.dot_general(
            table_ref[...], hot_ref[...], (((0,), (0,)), ((), ())), preferred_element_type=jnp.float32
        )

    def narrow(index, picked_ref):
        bundle, start, first_x, first_y = cells_of(index)
        off_y = first_y & (WIN - 1)
        off_x = first_x & (LANES - 1)
        lines = []
        for dy in range(TALL):
            parts = [picked_ref[dy * LANES + 8 * k : dy * LANES + 8 * k + 8] for k in range(LANES // 8)]
            parts.append(picked_ref[width + dy * HALO : width + (dy + 1) * HALO])
            lines.append(shift_rows(parts, off_x // 8, (8, 4, 2, 1), 2))
        low = shift_rows([line[0] for line in lines], off_y, (4, 2, 1), 4)
        high = shift_rows([line[1] for line in lines], off_y, (4, 2, 1), 4)
        patch = [shift_within(low[i], high[i], off_x)[:4].astype(jnp.int32) for i in range(4)]
        words = [(patch[i] << 16) | (patch[i + 2] & 0xFFFF) for i in range(2)]
        out_ref[bundle, :, pl.ds(start, step)] = jnp.concatenate(words, axis=0)

    total = bundles * per
    select(0, hot_a)

    def two(j, carry):
        select(2 * j + 1, hot_b)
        pick(hot_a, picked_a)
        narrow(jnp.maximum(2 * j - 1, 0), picked_b)
        select(jnp.minimum(2 * j + 2, total - 1), hot_a)
        pick(hot_b, picked_b)
        narrow(2 * j, picked_a)
        return carry

    lax.fori_loop(0, total // 2, two, 0)
    narrow(total - 1, picked_b)


def stencil_terms(patch, frac_x, frac_y):
    keep_y = 1.0 - frac_y
    level = keep_y * patch[1] + frac_y * patch[2]
    slope = (keep_y * (patch[2] - patch[0]) + frac_y * (patch[3] - patch[1])) * 0.5
    bend = keep_y * (patch[2] - 2.0 * patch[1] + patch[0]) + frac_y * (patch[3] - 2.0 * patch[2] + patch[1])
    keep_x = 1.0 - frac_x

    def across(rows):
        return [rows[k : k + 1] for k in range(4)]

    def flat(rows):
        return keep_x * rows[1] + frac_x * rows[2]

    def tilt(rows):
        return (keep_x * (rows[2] - rows[0]) + frac_x * (rows[3] - rows[1])) * 0.5

    def curve(rows):
        return keep_x * (rows[2] - 2.0 * rows[1] + rows[0]) + frac_x * (rows[3] - 2.0 * rows[2] + rows[1])

    level, slope, bend = across(level), across(slope), across(bend)
    return tilt(level), flat(slope), curve(level), flat(bend), tilt(slope)


def trace_kernel(
    tile_ref, slot_ref, fine_ref, root_ref, own_ref, one_ref, two_ref, three_ref, offset_ref,
    disp_ref, dist_ref, patch_ref, coarse_ref
):
    planes = tile_ref.shape[0]
    for k, ref in enumerate((own_ref, one_ref, two_ref, three_ref)):
        words = ref[...]
        half = words.shape[0]
        from_plane = (lax.axis_index("plane") + k) & (planes - 1)
        coarse_ref[from_plane, 0:half] = (words >> 16).astype(jnp.float32)
        coarse_ref[from_plane, half : 2 * half] = ((words << 16) >> 16).astype(jnp.float32)
    slots = tile_ref.shape[1]
    rays = slot_ref.shape[1]
    step = rays

    def one(index, carry):
        plane = index // (rays // step)
        start = pl.multiple_of((index % (rays // step)) * step, step)
        slot = slot_ref[pl.ds(plane, 1), pl.ds(start, step)]
        cell = fine_ref[pl.ds(plane, 1), pl.ds(start, step)]
        ids = lax.broadcasted_iota(jnp.int16, (slots, step), 0)
        onehot = jnp.where(ids == slot.astype(jnp.int16), jnp.bfloat16(1), jnp.bfloat16(0))
        picked = lax.dot_general(
            tile_ref[plane], onehot, (((0,), (0,)), ((), ())), preferred_element_type=jnp.float32
        )
        off_x = cell % TP - 1
        off_y = cell // TP - 1
        low = shift_rows([picked[TP * y : TP * y + 8] for y in range(TP)], off_y, (8, 4, 2, 1), 4)
        high = shift_rows([picked[TP * y + 8 : TP * y + 16] for y in range(TP)], off_y, (8, 4, 2, 1), 4)
        for i in range(4):
            first = jnp.where(off_x >= 8, high[i], low[i])
            patch_ref[plane, i, :, pl.ds(start, step)] = shift_within(first, high[i], off_x)
        return carry

    lax.fori_loop(0, planes * (rays // step), one, 0, unroll=True)

    offset = [offset_ref[0:1], offset_ref[1:2]]
    disp = [jnp.zeros((1, rays), jnp.float32)] * 2
    last = disp
    zero = jnp.zeros((1, rays), jnp.float32)
    unit = jnp.ones((1, rays), jnp.float32)
    dist = [unit, zero, zero, unit]
    before = dist
    for plane in range(planes):
        chi = float(FIRST + plane)
        ahead = 2.0 * chi / (chi + 1.0)
        behind = (chi - 1.0) / (chi + 1.0)
        strength = chi / (chi + 1.0)
        position = [offset[0] + disp[0], offset[1] + disp[1]]
        fine = stencil_terms([patch_ref[plane, i] for i in range(4)], position[0], position[1])
        cell = fine_ref[plane : plane + 1]
        root = root_ref[plane : plane + 1]
        base_x = ((root % 2) * (RATIO // 2) + cell % TP).astype(jnp.float32)
        base_y = ((root // 2) * (RATIO // 2) + cell // TP).astype(jnp.float32)
        coarse = stencil_terms(
            [coarse_ref[plane, 4 * i : 4 * i + 4] for i in range(4)],
            (base_x + position[0]) * (1.0 / RATIO),
            (base_y + position[1]) * (1.0 / RATIO),
        )
        once = UNIT / RATIO
        twice = UNIT / (RATIO * RATIO)
        grad_x = fine[0] + coarse[0] * once
        grad_y = fine[1] + coarse[1] * once
        xx = fine[2] + coarse[2] * twice
        yy = fine[3] + coarse[3] * twice
        xy = fine[4] + coarse[4] * twice
        new_disp = [
            ahead * disp[0] - behind * last[0] - strength * grad_x,
            ahead * disp[1] - behind * last[1] - strength * grad_y,
        ]
        product = [
            xx * dist[0] + xy * dist[2],
            xx * dist[1] + xy * dist[3],
            xy * dist[0] + yy * dist[2],
            xy * dist[1] + yy * dist[3],
        ]
        new_dist = [ahead * dist[k] - behind * before[k] - strength * product[k] for k in range(4)]
        disp, last, dist, before = new_disp, disp, new_dist, dist
    for k in range(2):
        disp_ref[k : k + 1] = disp[k]
    for k in range(4):
        dist_ref[k : k + 1] = dist[k]


def swap(array, axes):
    return lax.all_to_all(array, axes, split_axis=0, concat_axis=0, tiled=True)


def body(
    coarse_potential,
    fine_tiles,
    tile_requests,
    ray_slot,
    fine_cell,
    coarse_cell,
    tile_root,
    ray_offset,
):
    planes = lax.axis_size("plane")
    owners = lax.axis_size("ray")
    slots = tile_requests.shape[3]
    side = coarse_potential.shape[1]
    rays = ray_offset.shape[1]
    cells = TP * TP
    vmem = pl.BlockSpec(memory_space=pltpu.VMEM)

    def hop(array, by):
        return lax.ppermute(array, "plane", [(i, (i + by) % planes) for i in range(planes)])

    wishes = tile_requests[0].transpose(0, 2, 1).reshape(planes * slots, owners)
    wish_parts = [wishes] + [hop(wishes, k) for k in range(1, planes)]
    coarse_cell, *wish_parts = lax.optimization_barrier((coarse_cell, *wish_parts))
    size = coarse_potential.shape[0] * side // 2 // LANES
    message = pl.pallas_call(
        pack_kernel,
        out_shape=jax.ShapeDtypeStruct((owners * (size + 1), LANES), jnp.int32),
        in_specs=[vmem] * 5,
        out_specs=vmem,
        scratch_shapes=[pltpu.VMEM((LANES, LANES), jnp.int32)] * 2,
        name="pack",
    )(coarse_potential, *wish_parts)
    messages = swap(message.reshape(-1, 1, LANES), "ray").reshape(-1, LANES)
    at = lax.axis_index("plane")
    cell_rows = [lax.dynamic_slice(coarse_cell, ((at + k) % planes, 0), (1, rays)) for k in range(planes)]
    cell_parts = [cell_rows[0]] + [hop(cell_rows[k], k) for k in range(1, planes)]
    messages, *cell_parts = lax.optimization_barrier((messages, *cell_parts))

    outgoing = pl.pallas_call(
        take_kernel,
        out_shape=jax.ShapeDtypeStruct((planes, owners, slots, cells), jnp.bfloat16),
        in_specs=[vmem] * 2,
        out_specs=pl.BlockSpec(memory_space=pl.ANY),
        scratch_shapes=[
            pltpu.VMEM((LANES, owners), jnp.int32),
            pltpu.VMEM((planes, owners, slots, cells), jnp.bfloat16),
            pltpu.SemaphoreType.DMA((planes, owners // 4)),
        ],
        compiler_params=pltpu.CompilerParams(vmem_limit_bytes=32 << 20),
        cost_estimate=pl.CostEstimate(flops=1_100_000_000, bytes_accessed=1_600_000, transcendentals=0),
        name="take",
    )(messages, fine_tiles[0])
    arrived = swap(outgoing.reshape(planes * owners, slots, cells), ("plane", "ray"))

    codes = 2 * side // WIN * (side // LANES)
    step = min(512, rays)
    found = pl.pallas_call(
        coarse_kernel,
        out_shape=jax.ShapeDtypeStruct((planes, 8, rays), jnp.int32),
        in_specs=[vmem] * 5,
        out_specs=vmem,
        scratch_shapes=[
            pltpu.VMEM((codes, (TALL + 1) * LANES), jnp.bfloat16),
            pltpu.VMEM((planes, rays), jnp.int32),
            pltpu.VMEM((codes, step), jnp.bfloat16),
            pltpu.VMEM((codes, step), jnp.bfloat16),
            pltpu.VMEM(((TALL + 1) * LANES, step), jnp.float32),
            pltpu.VMEM(((TALL + 1) * LANES, step), jnp.float32),
        ],
        compiler_params=pltpu.CompilerParams(vmem_limit_bytes=32 << 20),
        cost_estimate=pl.CostEstimate(flops=6_000_000_000, bytes_accessed=1_500_000, transcendentals=0),
        name="coarse",
    )(messages, *cell_parts)
    found_parts = [found[0]] + [hop(found[k], planes - k) for k in range(1, planes)]

    return pl.pallas_call(
        trace_kernel,
        out_shape=(
            jax.ShapeDtypeStruct((2, rays), jnp.float32),
            jax.ShapeDtypeStruct((4, rays), jnp.float32),
        ),
        in_specs=[vmem] * 9,
        out_specs=(vmem,) * 2,
        scratch_shapes=[
            pltpu.VMEM((planes, 4, 8, rays), jnp.float32),
            pltpu.VMEM((planes, 16, rays), jnp.float32),
        ],
        compiler_params=pltpu.CompilerParams(vmem_limit_bytes=32 << 20),
        cost_estimate=pl.CostEstimate(flops=1_500_000_000, bytes_accessed=1_500_000, transcendentals=0),
        name="trace",
    )(
        arrived.reshape(planes, owners * slots, cells),
        ray_slot,
        fine_cell,
        tile_root,
        *found_parts,
        ray_offset,
    )


def solution(mesh):
    in_specs = (
        P(("plane", "ray"), None),
        P("plane", "ray", None),
        P(("plane", "ray"), None, None, None),
        P(None, ("plane", "ray")),
        P(None, ("plane", "ray")),
        P(None, ("plane", "ray")),
        P(None, ("plane", "ray")),
        P(None, ("plane", "ray")),
    )
    out_specs = (P(None, ("plane", "ray")), P(None, ("plane", "ray")))
    return jax.shard_map(body, mesh=mesh, in_specs=in_specs, out_specs=out_specs, check_vma=False)
```
